32 devices in a mesh: blk: 16 (over z, x, core), grp: 2 (over y).
Axes of the slice: x: 2, y: 2, z: 4, core: 2. Of those that a mesh axis runs over, the one named last changes fastest.
Arguments:
- spectra: float32 [1024, 2, 4, 512], P(('blk', 'grp')), may hold values from -120 to 120
- channel_ids: int32 [1024], replicated, may hold values from 0 to 1023, each once
- plan: int32 [16, 9], P('blk'), may hold values from 0 to 8, each once within a row
Outputs:
- correlations: bfloat16 [16, 9, 2, 64, 32, 400], P('blk', None, 'grp')
The draws below stay inside these ranges and needn't reach their ends.
Inputs may be any that keep to these rules, and one draw needn't show every extreme that they name: `channel_ids`: each channel number appears once. `plan`: each row holds every offset 0 to 8 once.
All inputs are finite; a program needn't handle non-finite values.
Results may differ from the reference program's by a relative error of at most 0.0068.
Values may be sent and summed in bfloat16 or wider, within the bound.
No kernel may reach another device: no remote copies, remote signals or barrier semaphores. Data moves between devices by JAX's collectives and lax.ppermute only.
A program may use at most 128 MiB of HBM per device.

```python
import math
import jax
import jax.numpy as jnp
from jax import lax

CHANNELS = 1024
SEGMENTS = 4
FREQS = 512
NFFT = 2000
HALF_LAG = 200
BLOCKS = 16
STEPS = 9
N_BLK = 16
N_GRP = 2


def draw_spectra(key, part):
    key_noise, key_level, key_colour = jax.random.split(key, 3)
    amplitude = jnp.exp(jax.random.uniform(key_level, (CHANNELS, 1, SEGMENTS, 1), minval=0.0, maxval=math.log(10.0)))
    colour = jnp.exp(jax.random.uniform(key_colour, (CHANNELS, 1, 1, FREQS), minval=math.log(0.3), maxval=math.log(3.0)))
    noise_part = jax.random.truncated_normal(key_noise, -4.0, 4.0, (CHANNELS, 2, SEGMENTS, FREQS))
    return (amplitude * colour * noise_part).astype(jnp.float32)


def setup_inputs(seed: int = 0) -> dict:
    keys = jax.random.split(jax.random.key(seed), 4)
    spectra = draw_spectra(jax.random.fold_in(keys[3], 71), 0)
    channel_ids = jax.random.permutation(keys[1], CHANNELS).astype(jnp.int32)
    plan = jax.vmap(lambda own: jax.random.permutation(own, STEPS))(jax.random.split(keys[2], BLOCKS)).reshape((BLOCKS, STEPS)).astype(jnp.int32)
    return dict(spectra=spectra, channel_ids=channel_ids, plan=plan)


def whiten(spectra):
    seg_power = lax.optimization_barrier(jnp.mean(spectra * spectra, axis=(1, 3)))
    whitened = spectra * lax.rsqrt(seg_power + 1e-06)[:, None, :, None]
    whitened = whitened.astype(jnp.bfloat16)
    return whitened.reshape(spectra.shape[0], 2 * spectra.shape[2], spectra.shape[3])

def lag_tables(freq_count):
    freq_axis = jnp.arange(freq_count, dtype=jnp.int32)
    lag_axis = jnp.arange(2 * HALF_LAG, dtype=jnp.int32) - HALF_LAG
    phase_index = freq_axis[:, None] * lag_axis[None, :] % NFFT
    angles = 2.0 * math.pi / NFFT * phase_index.astype(jnp.float32)
    weights = jnp.where(freq_axis == 0, 1.0, 2.0).astype(jnp.float32)[:, None]
    cos_tab = (weights * jnp.cos(angles)).astype(jnp.bfloat16)
    sin_tab = (-weights * jnp.sin(angles)).astype(jnp.bfloat16)
    return (cos_tab, sin_tab)

def reference(spectra, channel_ids, plan):
    whitened = whiten(spectra)
    cos_tab, sin_tab = lag_tables(FREQS)
    rotated = jnp.concatenate([whitened[:, SEGMENTS:], -whitened[:, :SEGMENTS]], axis=1)
    row_count = CHANNELS // N_BLK
    col_count = CHANNELS // (N_BLK * N_GRP)
    step_count = N_BLK // 2 + 1
    scaling = 1.0 / math.sqrt(2.0 * FREQS * SEGMENTS)

    def one_block(blk_index):
        row_start = blk_index * row_count
        rows_here = lax.dynamic_slice_in_dim(whitened, row_start, row_count, 0)
        rotated_here = lax.dynamic_slice_in_dim(rotated, row_start, row_count, 0)
        paired = jnp.stack([rows_here, rotated_here]).astype(jnp.float32)
        row_ids = lax.dynamic_slice_in_dim(channel_ids, row_start, row_count, 0)
        row_slots = row_start + jnp.arange(row_count, dtype=jnp.int32)

        def one_offset(offset):
            col_start = (blk_index + offset) % N_BLK * row_count
            columns = lax.dynamic_slice_in_dim(whitened, col_start, row_count, 0).astype(jnp.float32)
            col_ids = lax.dynamic_slice_in_dim(channel_ids, col_start, row_count, 0)
            col_slots = col_start + jnp.arange(row_count, dtype=jnp.int32)
            cross_spec = jnp.einsum('prsf,csf->prcf', paired, columns).astype(jnp.bfloat16)
            cross_spec = cross_spec.reshape(2, row_count * row_count, FREQS)
            real_part = jnp.dot(cross_spec[0], cos_tab, preferred_element_type=jnp.float32)
            imag_part = jnp.dot(cross_spec[1], sin_tab, preferred_element_type=jnp.float32)
            orient = jnp.where(row_ids[:, None] < col_ids[None, :], 1.0, -1.0).astype(jnp.float32).reshape(-1, 1)
            keeper = (row_slots[:, None] != col_slots[None, :]).astype(jnp.float32).reshape(-1, 1)
            lagged = ((real_part + orient * imag_part) * (scaling * keeper)).astype(jnp.bfloat16)
            lagged = lagged.reshape(row_count, N_GRP, col_count, 2 * HALF_LAG)
            return jnp.transpose(lagged, (1, 0, 2, 3))
        results = lax.map(one_offset, jnp.arange(step_count, dtype=jnp.int32))
        return jnp.take(results, plan[blk_index], axis=0)
    return lax.map(one_block, jnp.arange(N_BLK, dtype=jnp.int32))
```

```python
import functools
import math

import jax
import jax.numpy as jnp
from jax import lax
from jax.experimental import pallas as pl
from jax.experimental.pallas import tpu as pltpu
from jax.sharding import PartitionSpec as P

NFFT = 2000
HALF_LAG = 200
LANES = 128
PACK = 16


def passed_along(block, axis, distance):
    devices = range(lax.axis_size(axis))
    route = [((i - distance) % len(devices), i) for i in devices]
    return lax.ppermute(block, axis, route)


def whiten(spectra):
    seg_power = jnp.mean(spectra * spectra, axis=(1, 3))
    whitened = spectra * lax.rsqrt(seg_power + 1e-06)[:, None, :, None]
    whitened = whitened.astype(jnp.bfloat16)
    return whitened.reshape(spectra.shape[0], 2 * spectra.shape[2], spectra.shape[3])


def lag_tables(freq_count):
    freq_axis = jnp.arange(freq_count, dtype=jnp.int32)
    lag_axis = jnp.arange(2 * HALF_LAG, dtype=jnp.int32) - HALF_LAG
    phase_index = freq_axis[:, None] * lag_axis[None, :] % NFFT
    angles = 2.0 * math.pi / NFFT * phase_index.astype(jnp.float32)
    weights = jnp.where(freq_axis == 0, 1.0, 2.0).astype(jnp.float32)[:, None]
    cos_tab = (weights * jnp.cos(angles)).astype(jnp.bfloat16)
    sin_tab = (-weights * jnp.sin(angles)).astype(jnp.bfloat16)
    return (cos_tab, sin_tab)


def tree_sum(terms):
    while len(terms) > 1:
        paired = [a + b for a, b in zip(terms[::2], terms[1::2])]
        terms = paired + terms[len(terms) - len(terms) % 2:]
    return terms[0]


def correlate_kernel(info, row_ids, col_ids, table, own, partner, *rest, scale, chunk):
    out, rows, sign, cols, sems, cross_a, cross_b = rest[-7:]
    count = cols.shape[0]
    col_hbm = rest[:count]
    crosses = (cross_a, cross_b)
    parts, col_count, freq_count = own.shape
    seg_count = parts // 2
    row_count = rows.shape[0]
    step = pl.program_id(0)
    group = info[2 * count]

    def fetch(k):
        return pltpu.make_async_copy(col_hbm[k], cols.at[k], sems.at[k])

    @pl.when(step == 0)
    def _():
        for k in range(count):
            fetch(k).start()
        for source, first in ((own, group * col_count), (partner, (1 - group) * col_count)):
            for i in range(col_count):
                for s in range(parts):
                    line = source[s, i:i + 1, :]
                    rows[first + i, s] = jnp.broadcast_to(line, (PACK, freq_count))

    for k in range(count):
        @pl.when(step == k)
        def _():
            fetch(k).wait()

    ids = col_ids[0]

    def mark(i, carry):
        sign[i] = jnp.where(row_ids[i] < ids, 1.0, -1.0).astype(jnp.bfloat16)
        return carry

    lax.fori_loop(0, row_count, mark, 0)
    columns = cols.at[step]

    def form(cross, first):
        for tile in range(freq_count // LANES):
            lane = pl.ds(tile * LANES, LANES)
            c = [columns[s, :, lane] for s in range(parts)]
            for i in range(chunk):
                r = [jnp.concatenate([rows[first + i, s, :, lane]] * (col_count // PACK), axis=0) for s in range(parts)]
                re = tree_sum([r[s] * c[s] for s in range(parts)])
                im = tree_sum([r[seg_count + s] * c[s] - r[s] * c[seg_count + s] for s in range(seg_count)])
                here = pl.ds(i * col_count, col_count)
                cross[here, pl.ds(tile * LANES, LANES)] = re
                cross[here, pl.ds(freq_count + tile * LANES, LANES)] = im * sign[first + i]

    def transform(cross, first):
        lagged = jnp.dot(cross[...], table[...], preferred_element_type=jnp.float32) * scale
        out[0, 0, 0, pl.ds(first, chunk)] = lagged.astype(jnp.bfloat16).reshape(chunk, col_count, -1)

    form(crosses[0], 0)
    for k in range(row_count // chunk):
        if (k + 1) * chunk < row_count:
            form(crosses[(k + 1) % 2], (k + 1) * chunk)
        transform(crosses[k % 2], k * chunk)

    @pl.when(info[count + step] == 0)
    def _():
        for j in range(col_count):
            out[0, 0, 0, group * col_count + j, j:j + 1, :] = jnp.zeros((1, out.shape[-1]), jnp.bfloat16)


def correlate(info, row_ids, col_ids, table, own, partner, columns, output, step_count, scale):
    count = len(columns)
    parts, col_count, freq_count = own.shape
    row_count = 2 * col_count
    lag_count = table.shape[-1]
    kept = [] if output is None else [output]
    chunk = 32

    def whole(array):
        return pl.BlockSpec(array.shape, lambda d, *_: (0,) * array.ndim)

    return pl.pallas_call(
        functools.partial(correlate_kernel, scale=scale, chunk=chunk),
        grid_spec=pltpu.PrefetchScalarGridSpec(
            num_scalar_prefetch=2,
            grid=(count,),
            in_specs=[
                pl.BlockSpec((1, col_count, LANES), lambda d, *_: (d, 0, 0)),
                whole(table),
                whole(own),
                whole(partner),
            ] + [pl.BlockSpec(memory_space=pl.ANY)] * (count + len(kept)),
            out_specs=pl.BlockSpec(
                (1, 1, 1, row_count, col_count, lag_count),
                lambda d, info, _: (0, info[d], 0, 0, 0, 0),
            ),
            scratch_shapes=[
                pltpu.VMEM((row_count, parts, PACK, freq_count), jnp.bfloat16),
                pltpu.VMEM((row_count, col_count, LANES), jnp.bfloat16),
                pltpu.VMEM((count, parts, col_count, freq_count), jnp.bfloat16),
                pltpu.SemaphoreType.DMA((count,)),
                pltpu.VMEM((chunk * col_count, 2 * freq_count), jnp.bfloat16),
                pltpu.VMEM((chunk * col_count, 2 * freq_count), jnp.bfloat16),
            ],
        ),
        out_shape=jax.ShapeDtypeStruct((1, step_count, 1, row_count, col_count, lag_count), jnp.bfloat16),
        input_output_aliases={6 + count: 0} if kept else {},
        compiler_params=pltpu.CompilerParams(vmem_limit_bytes=56 << 20),
    )(info, row_ids, col_ids, table, own, partner, *columns, *kept)


def on_device_fused(spectra, channel_ids, plan):
    col_count, _, seg_count, freq_count = spectra.shape
    own = jnp.transpose(whiten(spectra), (1, 0, 2))
    partner = passed_along(own, "grp", 1)
    blk_count = lax.axis_size("blk")
    row_count = 2 * col_count
    step_count = blk_count // 2 + 1
    blk_index = lax.axis_index("blk")
    group = lax.axis_index("grp")
    odd = blk_index % 2 == 1

    even = [own, passed_along(own, "blk", -2), passed_along(own, "blk", -4)]
    while 2 * (len(even) - 1) < step_count - 1:
        even.append(passed_along(even[-1], "blk", -2) if len(even) % 2 else passed_along(even[-2], "blk", -4))
    columns = []
    for d in range(step_count):
        if d % 2 == 0:
            columns.append(even[d // 2])
        else:
            given = jnp.where(odd, even[d // 2], even[d // 2 + 1])
            columns.append(lax.ppermute(given, "blk", [(i ^ 1, i) for i in range(blk_count)]))

    cos_tab, sin_tab = lag_tables(freq_count)
    table = jnp.concatenate([cos_tab, sin_tab], axis=0)
    scale = 1.0 / math.sqrt(2.0 * freq_count * seg_count)
    row_ids = lax.dynamic_slice_in_dim(channel_ids, blk_index * row_count, row_count, 0)
    offsets = jnp.arange(step_count, dtype=jnp.int32)
    slots = jnp.sum(jnp.where(plan[0][None, :] == offsets[:, None], offsets[None, :], 0), axis=1)
    id_table = channel_ids.reshape(blk_count, lax.axis_size("grp"), col_count)[:, group]
    id_table = jnp.concatenate([id_table, id_table], axis=0)
    col_ids = lax.dynamic_slice_in_dim(id_table, blk_index, step_count, 0)
    col_ids = jnp.broadcast_to(col_ids[:, :, None], (step_count, col_count, LANES))

    output = None
    cuts = [0, 1, step_count // 2 + 1, step_count]
    for lo, hi in zip(cuts[:-1], cuts[1:]):
        info = jnp.concatenate([slots[lo:hi], offsets[lo:hi], group[None]])
        output = correlate(info, row_ids, col_ids[lo:hi], table, own, partner, columns[lo:hi], output, step_count, scale)
    return output


def on_device(spectra, channel_ids, plan):
    col_count = spectra.shape[0]
    seg_count = spectra.shape[2]
    freq_count = spectra.shape[3]
    whitened = whiten(spectra)
    row_block = lax.all_gather(whitened, "grp", axis=0, tiled=True)
    row_count = row_block.shape[0]
    rotated = jnp.concatenate([row_block[:, seg_count:], -row_block[:, :seg_count]], axis=1)
    paired = jnp.stack([row_block, rotated])
    blk_count = lax.axis_size("blk")
    step_count = blk_count // 2 + 1
    blk_index = lax.axis_index("blk")
    grp_index = lax.axis_index("grp")
    cos_tab, sin_tab = lag_tables(freq_count)
    lag_count = cos_tab.shape[1]
    row_start = blk_index * row_count
    row_ids = lax.dynamic_slice_in_dim(channel_ids, row_start, row_count, 0)
    row_slots = row_start + jnp.arange(row_count, dtype=jnp.int32)
    slot_list = jnp.arange(step_count, dtype=jnp.int32)
    scaling = 1.0 / math.sqrt(2.0 * freq_count * seg_count)

    def correlate_one(offset, columns, output):
        col_start = (blk_index + offset) % blk_count * row_count + grp_index * col_count
        col_ids = lax.dynamic_slice_in_dim(channel_ids, col_start, col_count, 0)
        col_slots = col_start + jnp.arange(col_count, dtype=jnp.int32)
        cross_spec = jnp.einsum(
            "prsf,csf->prcf", paired, columns, preferred_element_type=jnp.float32
        )
        cross_spec = cross_spec.astype(jnp.bfloat16).reshape(2, row_count * col_count, freq_count)
        real_part = jnp.dot(cross_spec[0], cos_tab, preferred_element_type=jnp.float32)
        imag_part = jnp.dot(cross_spec[1], sin_tab, preferred_element_type=jnp.float32)
        orient = (
            jnp.where(row_ids[:, None] < col_ids[None, :], 1.0, -1.0)
            .astype(jnp.float32)
            .reshape(-1, 1)
        )
        keeper = (row_slots[:, None] != col_slots[None, :]).astype(jnp.float32).reshape(-1, 1)
        lagged = ((real_part + orient * imag_part) * (scaling * keeper)).astype(jnp.bfloat16)
        lagged = lagged.reshape(1, 1, 1, row_count, col_count, lag_count)
        out_slot = jnp.sum(slot_list * (plan[0] == offset).astype(jnp.int32))
        return lax.dynamic_update_slice(output, lagged, (0, out_slot, 0, 0, 0, 0))

    output = jnp.zeros((1, step_count, 1, row_count, col_count, lag_count), jnp.bfloat16)

    def advance(offset, carry):
        columns, output = carry
        output = correlate_one(offset, columns, output)
        columns = passed_along(columns, "blk", -1)
        return (columns, output)

    columns, output = lax.fori_loop(0, step_count - 1, advance, (whitened, output))
    output = correlate_one(step_count - 1, columns, output)
    return output


def solution(mesh):
    blk_count, grp_count = mesh.shape["blk"], mesh.shape["grp"]

    def program(spectra, channel_ids, plan):
        col_count = spectra.shape[0] // (blk_count * grp_count)
        fused = col_count % (2 * PACK) == 0 and grp_count == 2 and blk_count % 8 == 0
        return jax.shard_map(
            on_device_fused if fused else on_device,
            mesh=mesh,
            in_specs=(P(("blk", "grp"), None, None, None), P(), P("blk", None)),
            out_specs=P("blk", None, "grp", None, None, None),
            check_vma=False,
        )(spectra, channel_ids, plan)

    return program
```

```python
import functools
import math

import jax
import jax.numpy as jnp
from jax import lax
from jax.experimental import pallas as pl
from jax.experimental.pallas import tpu as pltpu
from jax.sharding import PartitionSpec as P

NFFT = 2000
HALF_LAG = 200
LANES = 128
PACK = 16
TURN = 16
REST = 72
MIDDLE = 56
TOGETHER = 4
DELAY = 2
HELD_ROWS = 1024


def passed_along(block, axis, distance):
    devices = range(lax.axis_size(axis))
    route = [((i - distance) % len(devices), i) for i in devices]
    return lax.ppermute(block, axis, route)


def whiten(spectra):
    seg_power = jnp.mean(spectra * spectra, axis=(1, 3))
    whitened = spectra * lax.rsqrt(seg_power + 1e-06)[:, None, :, None]
    whitened = whitened.astype(jnp.bfloat16)
    return whitened.reshape(spectra.shape[0], 2 * spectra.shape[2], spectra.shape[3])


def lag_tables(freq_count):
    freq_axis = jnp.arange(freq_count, dtype=jnp.int32)
    lag_axis = jnp.arange(2 * HALF_LAG, dtype=jnp.int32) - HALF_LAG
    phase_index = freq_axis[:, None] * lag_axis[None, :] % NFFT
    angles = 2.0 * math.pi / NFFT * phase_index.astype(jnp.float32)
    weights = jnp.where(freq_axis == 0, 1.0, 2.0).astype(jnp.float32)[:, None]
    cos_tab = (weights * jnp.cos(angles)).astype(jnp.bfloat16)
    sin_tab = (-weights * jnp.sin(angles)).astype(jnp.bfloat16)
    return (cos_tab, sin_tab)


def tree_sum(terms):
    while len(terms) > 1:
        paired = [a + b for a, b in zip(terms[::2], terms[1::2])]
        terms = paired + terms[len(terms) - len(terms) % 2:]
    return terms[0]


def half_lag_tables(freq_count, scale):
    tile = lax.broadcasted_iota(jnp.int32, (2, freq_count, LANES), 0)
    freq = lax.broadcasted_iota(jnp.int32, (2, freq_count, LANES), 1)
    lane = lax.broadcasted_iota(jnp.int32, (2, freq_count, LANES), 2)
    wrapped = jnp.where(lane <= TURN, MIDDLE + LANES + lane, MIDDLE + lane)
    lag = jnp.where(tile == 0, wrapped, jnp.where(lane <= TURN, MIDDLE + lane, jnp.maximum(lane - REST, 0)))
    angles = 2.0 * math.pi / NFFT * (freq * lag % NFFT).astype(jnp.float32)
    weights = jnp.where(freq == 0, scale, 2.0 * scale)
    return (weights * jnp.cos(angles)).astype(jnp.bfloat16), (-weights * jnp.sin(angles)).astype(jnp.bfloat16)


def correlate_kernel(place, channels, plan, row_ids, cos_tab, sin_tab, own, partner, *rest, first, picks):
    out, rows, turn, cols, sems = rest[-5:]
    count = cols.shape[0]
    tiles, parts, col_count, _ = own.shape
    seg_count = parts // 2
    row_count = rows.shape[0]
    depth = 2 * LANES
    blk, group, blk_count = place[0], place[1], place[2]
    step = pl.program_id(0)

    def fetch(k):
        source, index = picks[k]
        array = rest[source] if index is None else rest[source].at[index]
        return pltpu.make_async_copy(array, cols.at[k], sems.at[k])

    @pl.when(step == 0)
    def _():
        for k in range(count):
            fetch(k).start()
        for source, start in ((own, group * col_count), (partner, (1 - group) * col_count)):
            def spread(n, carry, source=source, start=start):
                q, s = n // parts, n % parts
                for b in range(0, col_count, PACK):
                    lines = source[q, s, b:b + PACK, :]
                    for k in range(PACK):
                        rows[start + b + k, q, s] = jnp.broadcast_to(lines[k:k + 1, :], (PACK, LANES))
                return carry

            lax.fori_loop(0, tiles * parts, spread, 0)

    for k in range(count):
        @pl.when(step == k)
        def _(k=k):
            fetch(k).wait()

    id_line = row_ids[0]
    col_start = (blk + first + step) % blk_count * row_count + group * col_count
    for j in range(col_count):
        turn[j:j + 1, :] = jnp.where(id_line < channels[col_start + j], 1.0, -1.0)

    lane = lax.broadcasted_iota(jnp.int32, (col_count, LANES), 1)
    low = lane <= TURN
    late = lane >= REST
    mirror = (TURN - lane) & (LANES - 1)

    def form(c, i, tile):
        r = [jnp.concatenate([rows[i, tile, s]] * (col_count // PACK), axis=0) for s in range(parts)]
        re = tree_sum([r[s] * c[s] for s in range(parts)])
        im = tree_sum([r[seg_count + s] * c[s] - r[s] * c[seg_count + s] for s in range(seg_count)])
        return re, im

    def push(h):
        deep = pl.ds(h * depth, depth)
        for unit, tab in enumerate((cos_tab, sin_tab)):
            side = jnp.concatenate([tab[0, deep, :], tab[1, deep, :]], axis=1)
            pltpu.matmul_push_rhs(side, staging_register=h % 2, mxu_index=unit)

    def finish(i, even, odd):
        sign = jnp.broadcast_to(turn[:, i:i + 1], (col_count, LANES))
        odd_u, odd_v = odd[:, :LANES] * sign, odd[:, LANES:] * sign
        even_u, even_v = even[:, :LANES], even[:, LANES:]
        ahead_u = (even_u + odd_u).astype(jnp.bfloat16)
        ahead_v = (even_v + odd_v).astype(jnp.bfloat16)
        back_u = jnp.take_along_axis(even_u - odd_u, mirror, axis=1, mode="promise_in_bounds")
        back_v = jnp.take_along_axis(even_v - odd_v, mirror, axis=1, mode="promise_in_bounds")
        line = out.at[0, 0, 0, i]
        line[:, 0:LANES] = back_u.astype(jnp.bfloat16)
        line[:, LANES:2 * LANES] = jnp.where(late, ahead_v, back_v.astype(jnp.bfloat16))
        line[:, 2 * LANES:3 * LANES] = jnp.where(low, ahead_v, ahead_u)
        line[:, 3 * LANES:] = ahead_u[:, :out.shape[-1] - 3 * LANES]

    def multiply(*sums):
        held = len(sums) // 2
        sums_even, sums_odd = sums[:held], sums[held:]
        halves = tiles // 2
        push(0)
        for block in range(0, row_count, held):
            for h in range(halves):
                if h + 1 < halves or block + held < row_count:
                    push((h + 1) % halves)
                for g0 in range(0, held, TOGETHER):
                    formed = []
                    for tile in (2 * h, 2 * h + 1):
                        c = [cols[step, tile, s] for s in range(parts)]
                        formed.append([form(c, block + g0 + k, tile) for k in range(TOGETHER)])
                    for k in range(TOGETHER):
                        g = g0 + k
                        fresh = h % 2 if g == 0 else None
                        for part, held_sums in enumerate((sums_even, sums_odd)):
                            side = jnp.concatenate([formed[0][k][part], formed[1][k][part]], axis=1)
                            pltpu.matmul_acc_lhs(held_sums[g], side, load_staged_rhs=fresh)
                        if h == halves - 1 and g >= DELAY:
                            finish(block + g - DELAY, pltpu.matmul_pop(sums_even[g - DELAY]), pltpu.matmul_pop(sums_odd[g - DELAY]))
            for g in range(held - DELAY, held):
                finish(block + g, pltpu.matmul_pop(sums_even[g]), pltpu.matmul_pop(sums_odd[g]))

    held = min(row_count, HELD_ROWS // col_count)
    pl.run_scoped(
        multiply,
        *[pltpu.ACC(0)((col_count, depth), jnp.float32)] * held,
        *[pltpu.ACC(1)((col_count, depth), jnp.float32)] * held,
    )

    if first == 0:
        @pl.when(step == 0)
        def _():
            for j in range(col_count):
                out[0, 0, 0, group * col_count + j, j:j + 1, :] = jnp.zeros((1, out.shape[-1]), jnp.bfloat16)


def correlate(place, channels, plan, row_ids, tables, own, partner, arrays, picks, first, output, step_count):
    count = len(picks)
    tiles, parts, col_count, _ = own.shape
    row_count = 2 * col_count
    lag_count = 2 * HALF_LAG
    kept = [] if output is None else [output]

    def whole(array):
        return pl.BlockSpec(array.shape, lambda d, *_: (0,) * array.ndim)

    def slot(d, place, channels, plan):
        return (0, sum(jnp.where(plan[0, t] == first + d, t, 0) for t in range(step_count)), 0, 0, 0, 0)

    pairs = count * row_count * col_count * tiles * LANES
    return pl.pallas_call(
        functools.partial(correlate_kernel, first=first, picks=picks),
        grid_spec=pltpu.PrefetchScalarGridSpec(
            num_scalar_prefetch=3,
            grid=(count,),
            in_specs=[
                pl.BlockSpec((1, 1, row_count), lambda d, place, *_: (place[0], 0, 0)),
                whole(tables[0]),
                whole(tables[1]),
                whole(own),
                whole(partner),
            ] + [pl.BlockSpec(memory_space=pl.ANY)] * (len(arrays) + len(kept)),
            out_specs=pl.BlockSpec((1, 1, 1, row_count, col_count, lag_count), slot),
            scratch_shapes=[
                pltpu.VMEM((row_count, tiles, parts, PACK, LANES), jnp.bfloat16),
                pltpu.VMEM((col_count, row_count), jnp.float32),
                pltpu.VMEM((count, tiles, parts, col_count, LANES), jnp.bfloat16),
                pltpu.SemaphoreType.DMA((count,)),
            ],
        ),
        out_shape=jax.ShapeDtypeStruct((1, step_count, 1, row_count, col_count, lag_count), jnp.bfloat16),
        input_output_aliases={8 + len(arrays): 0} if kept else {},
        cost_estimate=pl.CostEstimate(flops=1600 * pairs, bytes_accessed=count * 3000000, transcendentals=0),
        compiler_params=pltpu.CompilerParams(vmem_limit_bytes=56 << 20),
    )(place, channels, plan, row_ids, *tables, own, partner, *arrays, *kept)


def whiten_tiles(spectra):
    whitened = whiten(spectra)
    channels, parts, freq_count = whitened.shape
    return jnp.transpose(whitened.reshape(channels, parts, freq_count // LANES, LANES), (2, 1, 0, 3))


def on_device_fused(spectra, channel_ids, plan):
    col_count, _, seg_count, freq_count = spectra.shape
    blk_count = lax.axis_size("blk")
    row_count = 2 * col_count
    step_count = blk_count // 2 + 1
    blk_index = lax.axis_index("blk")
    group = lax.axis_index("grp")
    odd = blk_index % 2 == 1
    place = jnp.stack([blk_index, group, jnp.int32(blk_count)])
    row_ids = channel_ids.reshape(blk_count, 1, row_count)

    own = whiten_tiles(spectra)
    partner = passed_along(own, "grp", 1)
    near, far = passed_along(own, "blk", -2), passed_along(own, "blk", -4)
    tables = half_lag_tables(freq_count, 1.0 / math.sqrt(2.0 * freq_count * seg_count))

    def stage(arrays, picks, first, output):
        return correlate(place, channel_ids, plan, row_ids, tables, own, partner, arrays, picks, first, output, step_count)

    output = stage([own], [(0, None)], 0, None)
    even = own
    for first in range(1, step_count, 4):
        near, far, output = lax.optimization_barrier((near, far, output))
        if first + 4 < step_count:
            later = passed_along(far, "blk", -2), passed_along(far, "blk", -4)
        given = jnp.where(odd, jnp.stack([even, near]), jnp.stack([near, far]))
        taken = lax.ppermute(given, "blk", [(i ^ 1, i) for i in range(blk_count)])
        output = stage([taken, near, far], [(0, 0), (1, None), (0, 1), (2, None)], first, output)
        even, (near, far) = far, later
    return output


def on_device(spectra, channel_ids, plan):
    col_count = spectra.shape[0]
    seg_count = spectra.shape[2]
    freq_count = spectra.shape[3]
    whitened = whiten(spectra)
    row_block = lax.all_gather(whitened, "grp", axis=0, tiled=True)
    row_count = row_block.shape[0]
    rotated = jnp.concatenate([row_block[:, seg_count:], -row_block[:, :seg_count]], axis=1)
    paired = jnp.stack([row_block, rotated])
    blk_count = lax.axis_size("blk")
    step_count = blk_count // 2 + 1
    blk_index = lax.axis_index("blk")
    grp_index = lax.axis_index("grp")
    cos_tab, sin_tab = lag_tables(freq_count)
    lag_count = cos_tab.shape[1]
    row_start = blk_index * row_count
    row_ids = lax.dynamic_slice_in_dim(channel_ids, row_start, row_count, 0)
    row_slots = row_start + jnp.arange(row_count, dtype=jnp.int32)
    slot_list = jnp.arange(step_count, dtype=jnp.int32)
    scaling = 1.0 / math.sqrt(2.0 * freq_count * seg_count)

    def correlate_one(offset, columns, output):
        col_start = (blk_index + offset) % blk_count * row_count + grp_index * col_count
        col_ids = lax.dynamic_slice_in_dim(channel_ids, col_start, col_count, 0)
        col_slots = col_start + jnp.arange(col_count, dtype=jnp.int32)
        cross_spec = jnp.einsum(
            "prsf,csf->prcf", paired, columns, preferred_element_type=jnp.float32
        )
        cross_spec = cross_spec.astype(jnp.bfloat16).reshape(2, row_count * col_count, freq_count)
        real_part = jnp.dot(cross_spec[0], cos_tab, preferred_element_type=jnp.float32)
        imag_part = jnp.dot(cross_spec[1], sin_tab, preferred_element_type=jnp.float32)
        orient = (
            jnp.where(row_ids[:, None] < col_ids[None, :], 1.0, -1.0)
            .astype(jnp.float32)
            .reshape(-1, 1)
        )
        keeper = (row_slots[:, None] != col_slots[None, :]).astype(jnp.float32).reshape(-1, 1)
        lagged = ((real_part + orient * imag_part) * (scaling * keeper)).astype(jnp.bfloat16)
        lagged = lagged.reshape(1, 1, 1, row_count, col_count, lag_count)
        out_slot = jnp.sum(slot_list * (plan[0] == offset).astype(jnp.int32))
        return lax.dynamic_update_slice(output, lagged, (0, out_slot, 0, 0, 0, 0))

    output = jnp.zeros((1, step_count, 1, row_count, col_count, lag_count), jnp.bfloat16)

    def advance(offset, carry):
        columns, output = carry
        output = correlate_one(offset, columns, output)
        columns = passed_along(columns, "blk", -1)
        return (columns, output)

    columns, output = lax.fori_loop(0, step_count - 1, advance, (whitened, output))
    output = correlate_one(step_count - 1, columns, output)
    return output


def solution(mesh):
    blk_count, grp_count = mesh.shape["blk"], mesh.shape["grp"]

    def program(spectra, channel_ids, plan):
        col_count = spectra.shape[0] // (blk_count * grp_count)
        fused = col_count == 2 * PACK and grp_count == 2 and blk_count % 8 == 0
        fused = fused and spectra.shape[3] % (4 * LANES) == 0
        return jax.shard_map(
            on_device_fused if fused else on_device,
            mesh=mesh,
            in_specs=(P(("blk", "grp"), None, None, None), P(), P("blk", None)),
            out_specs=P("blk", None, "grp", None, None, None),
            check_vma=False,
        )(spectra, channel_ids, plan)

    return program
```

```python
import functools
import math

import jax
import jax.numpy as jnp
from jax import lax
from jax.experimental import pallas as pl
from jax.experimental.pallas import tpu as pltpu
from jax.sharding import PartitionSpec as P

NFFT = 2000
HALF_LAG = 200
LANES = 128
PACK = 16
TURN = 16
REST = 72
MIDDLE = 56
TOGETHER = 8
DELAY = 2


def passed_along(block, axis, distance):
    devices = range(lax.axis_size(axis))
    route = [((i - distance) % len(devices), i) for i in devices]
    return lax.ppermute(block, axis, route)


def whiten(spectra):
    seg_power = jnp.mean(spectra * spectra, axis=(1, 3))
    whitened = spectra * lax.rsqrt(seg_power + 1e-06)[:, None, :, None]
    whitened = whitened.astype(jnp.bfloat16)
    return whitened.reshape(spectra.shape[0], 2 * spectra.shape[2], spectra.shape[3])


def lag_tables(freq_count):
    freq_axis = jnp.arange(freq_count, dtype=jnp.int32)
    lag_axis = jnp.arange(2 * HALF_LAG, dtype=jnp.int32) - HALF_LAG
    phase_index = freq_axis[:, None] * lag_axis[None, :] % NFFT
    angles = 2.0 * math.pi / NFFT * phase_index.astype(jnp.float32)
    weights = jnp.where(freq_axis == 0, 1.0, 2.0).astype(jnp.float32)[:, None]
    cos_tab = (weights * jnp.cos(angles)).astype(jnp.bfloat16)
    sin_tab = (-weights * jnp.sin(angles)).astype(jnp.bfloat16)
    return (cos_tab, sin_tab)


def tree_sum(terms):
    while len(terms) > 1:
        paired = [a + b for a, b in zip(terms[::2], terms[1::2])]
        terms = paired + terms[len(terms) - len(terms) % 2:]
    return terms[0]


def half_lag_tables(freq_count, scale):
    tile = lax.broadcasted_iota(jnp.int32, (2, 1, 1, LANES), 0)
    lane = lax.broadcasted_iota(jnp.int32, (2, 1, 1, LANES), 3)
    wrapped = jnp.where(lane <= TURN, MIDDLE + LANES + lane, MIDDLE + lane)
    lag = jnp.where(tile == 0, wrapped, jnp.where(lane <= TURN, MIDDLE + lane, jnp.maximum(lane - REST, 0)))
    coarse = PACK * jnp.arange(freq_count // PACK, dtype=jnp.int32)[None, :, None, None]
    fine = jnp.arange(PACK, dtype=jnp.int32)[None, None, :, None]

    def turned(freq):
        angles = 2.0 * math.pi / NFFT * (freq * lag % NFFT).astype(jnp.float32)
        return jnp.cos(angles), jnp.sin(angles)

    (cos_a, sin_a), (cos_b, sin_b) = lax.optimization_barrier((turned(coarse), turned(fine)))
    weights = jnp.where(coarse + fine == 0, scale, 2.0 * scale)
    cos_tab = (weights * (cos_a * cos_b - sin_a * sin_b)).astype(jnp.bfloat16)
    sin_tab = (-weights * (sin_a * cos_b + cos_a * sin_b)).astype(jnp.bfloat16)
    return cos_tab.reshape(2, freq_count, LANES), sin_tab.reshape(2, freq_count, LANES)


def correlate_kernel(channels, plan, ids, cos_tab, sin_tab, own, partner, *rest, first, picks):
    out, rows, turn, cols, sems = rest[-5:]
    count = cols.shape[0]
    tiles, parts, col_count, _ = own.shape
    seg_count = parts // 2
    row_count = 2 * col_count
    depth = 2 * LANES
    blk, group, blk_count = lax.axis_index("blk"), lax.axis_index("grp"), lax.axis_size("blk")
    step, half = pl.program_id(0), pl.program_id(1)

    def fetch(k, parity):
        return pltpu.make_async_copy(rest[picks[k][parity]], cols.at[k], sems.at[k])

    @pl.when((step == 0) & (half == 0))
    def _():
        for parity in range(2):
            @pl.when(blk % 2 == parity)
            def _(parity=parity):
                for k in range(count):
                    fetch(k, parity).start()
        for source, place in ((own, group), (partner, 1 - group)):
            for q in range(tiles):
                rows[place, q] = source[q]

    for k in range(count):
        @pl.when((step == k) & (half == 0))
        def _(k=k):
            fetch(k, 0).wait()

    row_start = blk * row_count + half * col_count
    line = jnp.broadcast_to(ids[pl.ds(row_start // LANES, 1), :], (8, LANES))
    id_line = pltpu.roll(line, (LANES - row_start % LANES) % LANES, 1)[0:1, :]
    col_start = (blk + first + step) % blk_count * row_count + group * col_count
    for j in range(col_count):
        turn[j:j + 1, :] = jnp.where(id_line < channels[col_start + j], 1.0, -1.0)

    lane = lax.broadcasted_iota(jnp.int32, (col_count, LANES), 1)
    low = lane <= TURN
    late = lane >= REST
    mirror = (TURN - lane) & (LANES - 1)

    def form(c, i, tile):
        b = i // PACK * PACK
        lines = [rows[half, tile, s, b:b + PACK, :] for s in range(parts)]
        r = [jnp.broadcast_to(v[i - b:i - b + 1, :], (col_count, LANES)) for v in lines]
        re = tree_sum([r[s] * c[s] for s in range(parts)])
        im = tree_sum([r[seg_count + s] * c[s] - r[s] * c[seg_count + s] for s in range(seg_count)])
        return re, im

    def push(h):
        deep = pl.ds(h * depth, depth)
        for unit, tab in enumerate((cos_tab, sin_tab)):
            side = jnp.concatenate([tab[0, deep, :], tab[1, deep, :]], axis=1)
            pltpu.matmul_push_rhs(side, staging_register=h % 2, mxu_index=unit)

    def finish(i, even, odd):
        sign = jnp.broadcast_to(turn[:, i:i + 1], (col_count, LANES))
        odd_u, odd_v = odd[:, :LANES] * sign, odd[:, LANES:] * sign
        even_u, even_v = even[:, :LANES], even[:, LANES:]
        ahead_u = (even_u + odd_u).astype(jnp.bfloat16)
        ahead_v = (even_v + odd_v).astype(jnp.bfloat16)
        back_u = jnp.take_along_axis(even_u - odd_u, mirror, axis=1, mode="promise_in_bounds")
        back_v = jnp.take_along_axis(even_v - odd_v, mirror, axis=1, mode="promise_in_bounds")
        line = out.at[0, 0, 0, i]
        line[:, 0:LANES] = back_u.astype(jnp.bfloat16)
        line[:, LANES:2 * LANES] = jnp.where(late, ahead_v, back_v.astype(jnp.bfloat16))
        line[:, 2 * LANES:3 * LANES] = jnp.where(low, ahead_v, ahead_u)
        line[:, 3 * LANES:] = ahead_u[:, :out.shape[-1] - 3 * LANES]

    def multiply(*sums):
        sums_even, sums_odd = sums[:col_count], sums[col_count:]
        push(0)
        for h in range(tiles // 2):
            if h + 1 < tiles // 2:
                push(h + 1)
            for g0 in range(0, col_count, TOGETHER):
                formed = []
                for tile in (2 * h, 2 * h + 1):
                    c = [cols[step, tile, s] for s in range(parts)]
                    formed.append([form(c, g0 + k, tile) for k in range(TOGETHER)])
                for k in range(TOGETHER):
                    g = g0 + k
                    fresh = h % 2 if g == 0 else None
                    for part, held in enumerate((sums_even, sums_odd)):
                        side = jnp.concatenate([formed[0][k][part], formed[1][k][part]], axis=1)
                        pltpu.matmul_acc_lhs(held[g], side, load_staged_rhs=fresh)
                    if h + 1 == tiles // 2 and g >= DELAY:
                        finish(g - DELAY, pltpu.matmul_pop(sums_even[g - DELAY]), pltpu.matmul_pop(sums_odd[g - DELAY]))
        for g in range(col_count - DELAY, col_count):
            finish(g, pltpu.matmul_pop(sums_even[g]), pltpu.matmul_pop(sums_odd[g]))

    pl.run_scoped(
        multiply,
        *[pltpu.ACC(0)((col_count, depth), jnp.float32)] * col_count,
        *[pltpu.ACC(1)((col_count, depth), jnp.float32)] * col_count,
    )

    if first == 0:
        @pl.when((step == 0) & (half == group))
        def _():
            for j in range(col_count):
                out[0, 0, 0, j, j:j + 1, :] = jnp.zeros((1, out.shape[-1]), jnp.bfloat16)


def correlate(channels, plan, ids, tables, own, partner, arrays, picks, first, output, step_count):
    count = len(picks)
    tiles, parts, col_count, _ = own.shape
    lag_count = 2 * HALF_LAG
    kept = [] if output is None else [output]

    def whole(array):
        return pl.BlockSpec(array.shape, lambda *_: (0,) * array.ndim)

    def slot(d, half, channels, plan):
        return (0, sum(jnp.where(plan[0, t] == first + d, t, 0) for t in range(step_count)), 0, half, 0, 0)

    pairs = count * 2 * col_count * col_count * tiles * LANES
    return pl.pallas_call(
        functools.partial(correlate_kernel, first=first, picks=picks),
        grid_spec=pltpu.PrefetchScalarGridSpec(
            num_scalar_prefetch=2,
            grid=(count, 2),
            in_specs=[whole(ids), whole(tables[0]), whole(tables[1]), whole(own), whole(partner)]
            + [pl.BlockSpec(memory_space=pl.ANY)] * (len(arrays) + len(kept)),
            out_specs=pl.BlockSpec((1, 1, 1, col_count, col_count, lag_count), slot),
            scratch_shapes=[
                pltpu.VMEM((2, tiles, parts, col_count, LANES), jnp.bfloat16),
                pltpu.VMEM((col_count, LANES), jnp.float32),
                pltpu.VMEM((count, tiles, parts, col_count, LANES), jnp.bfloat16),
                pltpu.SemaphoreType.DMA((count,)),
            ],
        ),
        out_shape=jax.ShapeDtypeStruct((1, step_count, 1, 2 * col_count, col_count, lag_count), jnp.bfloat16),
        input_output_aliases={7 + len(arrays): 0} if kept else {},
        cost_estimate=pl.CostEstimate(flops=1600 * pairs, bytes_accessed=count * 3000000, transcendentals=0),
        compiler_params=pltpu.CompilerParams(vmem_limit_bytes=40 << 20),
    )(channels, plan, ids, *tables, own, partner, *arrays, *kept)


def whiten_tiles(spectra):
    whitened = whiten(spectra)
    channels, parts, freq_count = whitened.shape
    return jnp.transpose(whitened.reshape(channels, parts, freq_count // LANES, LANES), (2, 1, 0, 3))


def on_device_fused(spectra, channel_ids, plan):
    col_count, _, seg_count, freq_count = spectra.shape
    blk_count = lax.axis_size("blk")
    step_count = blk_count // 2 + 1
    ids = channel_ids.reshape(-1, LANES)

    def other_core(block):
        return lax.ppermute(block, "blk", [(i ^ 1, i) for i in range(blk_count)])

    own = whiten_tiles(spectra)
    partner = passed_along(own, "grp", 1)
    tables = half_lag_tables(freq_count, 1.0 / math.sqrt(2.0 * freq_count * seg_count))
    sent, tables = lax.optimization_barrier((own, tables))
    near, far = passed_along(sent, "blk", -2), passed_along(sent, "blk", -4)

    def stage(arrays, picks, first, output):
        return correlate(channel_ids, plan, ids, tables, own, partner, arrays, picks, first, output, step_count)

    output = stage([own], [(0, 0)], 0, None)
    last = own
    for first in range(1, step_count, 4):
        near, far, last, output = lax.optimization_barrier((near, far, last, output))
        if first + 4 < step_count:
            later = passed_along(far, "blk", -2), passed_along(far, "blk", -4)
        taken = other_core(last) if first == 1 else crossed
        crossed = other_core(far)
        arrays = [near, far, taken, other_core(near), crossed]
        output = stage(arrays, [(2, 3), (0, 0), (3, 4), (1, 1)], first, output)
        last, (near, far) = far, later
    return output


def on_device(spectra, channel_ids, plan):
    col_count = spectra.shape[0]
    seg_count = spectra.shape[2]
    freq_count = spectra.shape[3]
    whitened = whiten(spectra)
    row_block = lax.all_gather(whitened, "grp", axis=0, tiled=True)
    row_count = row_block.shape[0]
    rotated = jnp.concatenate([row_block[:, seg_count:], -row_block[:, :seg_count]], axis=1)
    paired = jnp.stack([row_block, rotated])
    blk_count = lax.axis_size("blk")
    step_count = blk_count // 2 + 1
    blk_index = lax.axis_index("blk")
    grp_index = lax.axis_index("grp")
    cos_tab, sin_tab = lag_tables(freq_count)
    lag_count = cos_tab.shape[1]
    row_start = blk_index * row_count
    row_ids = lax.dynamic_slice_in_dim(channel_ids, row_start, row_count, 0)
    row_slots = row_start + jnp.arange(row_count, dtype=jnp.int32)
    slot_list = jnp.arange(step_count, dtype=jnp.int32)
    scaling = 1.0 / math.sqrt(2.0 * freq_count * seg_count)

    def correlate_one(offset, columns, output):
        col_start = (blk_index + offset) % blk_count * row_count + grp_index * col_count
        col_ids = lax.dynamic_slice_in_dim(channel_ids, col_start, col_count, 0)
        col_slots = col_start + jnp.arange(col_count, dtype=jnp.int32)
        cross_spec = jnp.einsum(
            "prsf,csf->prcf", paired, columns, preferred_element_type=jnp.float32
        )
        cross_spec = cross_spec.astype(jnp.bfloat16).reshape(2, row_count * col_count, freq_count)
        real_part = jnp.dot(cross_spec[0], cos_tab, preferred_element_type=jnp.float32)
        imag_part = jnp.dot(cross_spec[1], sin_tab, preferred_element_type=jnp.float32)
        orient = (
            jnp.where(row_ids[:, None] < col_ids[None, :], 1.0, -1.0)
            .astype(jnp.float32)
            .reshape(-1, 1)
        )
        keeper = (row_slots[:, None] != col_slots[None, :]).astype(jnp.float32).reshape(-1, 1)
        lagged = ((real_part + orient * imag_part) * (scaling * keeper)).astype(jnp.bfloat16)
        lagged = lagged.reshape(1, 1, 1, row_count, col_count, lag_count)
        out_slot = jnp.sum(slot_list * (plan[0] == offset).astype(jnp.int32))
        return lax.dynamic_update_slice(output, lagged, (0, out_slot, 0, 0, 0, 0))

    output = jnp.zeros((1, step_count, 1, row_count, col_count, lag_count), jnp.bfloat16)

    def advance(offset, carry):
        columns, output = carry
        output = correlate_one(offset, columns, output)
        columns = passed_along(columns, "blk", -1)
        return (columns, output)

    columns, output = lax.fori_loop(0, step_count - 1, advance, (whitened, output))
    output = correlate_one(step_count - 1, columns, output)
    return output


def solution(mesh):
    blk_count, grp_count = mesh.shape["blk"], mesh.shape["grp"]

    def program(spectra, channel_ids, plan):
        col_count = spectra.shape[0] // (blk_count * grp_count)
        fused = col_count == 2 * PACK and grp_count == 2 and blk_count % 8 == 0
        fused = fused and spectra.shape[3] % (4 * LANES) == 0
        return jax.shard_map(
            on_device_fused if fused else on_device,
            mesh=mesh,
            in_specs=(P(("blk", "grp"), None, None, None), P(), P("blk", None)),
            out_specs=P("blk", None, "grp", None, None, None),
            check_vma=False,
        )(spectra, channel_ids, plan)

    return program
```

```python
import functools
import math

import jax
import jax.numpy as jnp
from jax import lax
from jax.experimental import pallas as pl
from jax.experimental.pallas import tpu as pltpu
from jax.sharding import PartitionSpec as P

NFFT = 2000
HALF_LAG = 200
LANES = 128
PACK = 16
TURN = 16
REST = 72
MIDDLE = 56
TOGETHER = 8
DELAY = 2


def passed_along(block, axis, distance):
    devices = range(lax.axis_size(axis))
    route = [((i - distance) % len(devices), i) for i in devices]
    return lax.ppermute(block, axis, route)


def whiten(spectra):
    seg_power = jnp.mean(spectra * spectra, axis=(1, 3))
    whitened = spectra * lax.rsqrt(seg_power + 1e-06)[:, None, :, None]
    whitened = whitened.astype(jnp.bfloat16)
    return whitened.reshape(spectra.shape[0], 2 * spectra.shape[2], spectra.shape[3])


def lag_tables(freq_count):
    freq_axis = jnp.arange(freq_count, dtype=jnp.int32)
    lag_axis = jnp.arange(2 * HALF_LAG, dtype=jnp.int32) - HALF_LAG
    phase_index = freq_axis[:, None] * lag_axis[None, :] % NFFT
    angles = 2.0 * math.pi / NFFT * phase_index.astype(jnp.float32)
    weights = jnp.where(freq_axis == 0, 1.0, 2.0).astype(jnp.float32)[:, None]
    cos_tab = (weights * jnp.cos(angles)).astype(jnp.bfloat16)
    sin_tab = (-weights * jnp.sin(angles)).astype(jnp.bfloat16)
    return (cos_tab, sin_tab)


def tree_sum(terms):
    while len(terms) > 1:
        paired = [a + b for a, b in zip(terms[::2], terms[1::2])]
        terms = paired + terms[len(terms) - len(terms) % 2:]
    return terms[0]


def half_lag_tables(freq_count, scale):
    tile = lax.broadcasted_iota(jnp.int32, (2, 1, 1, LANES), 0)
    lane = lax.broadcasted_iota(jnp.int32, (2, 1, 1, LANES), 3)
    wrapped = jnp.where(lane <= TURN, MIDDLE + LANES + lane, MIDDLE + lane)
    lag = jnp.where(tile == 0, wrapped, jnp.where(lane <= TURN, MIDDLE + lane, jnp.maximum(lane - REST, 0)))
    coarse = PACK * jnp.arange(freq_count // PACK, dtype=jnp.int32)[None, :, None, None]
    fine = jnp.arange(PACK, dtype=jnp.int32)[None, None, :, None]

    def turned(freq):
        angles = 2.0 * math.pi / NFFT * (freq * lag % NFFT).astype(jnp.float32)
        return jnp.cos(angles), jnp.sin(angles)

    (cos_a, sin_a), (cos_b, sin_b) = lax.optimization_barrier((turned(coarse), turned(fine)))
    weights = jnp.where(coarse + fine == 0, scale, 2.0 * scale)
    cos_tab = (weights * (cos_a * cos_b - sin_a * sin_b)).astype(jnp.bfloat16)
    sin_tab = (-weights * (sin_a * cos_b + cos_a * sin_b)).astype(jnp.bfloat16)
    return cos_tab.reshape(2, freq_count, LANES), sin_tab.reshape(2, freq_count, LANES)


def correlate_kernel(info, ids, cos_tab, sin_tab, own, partner, *rest, first, picks):
    out, rows, turn, cols, sems = rest[-5:]
    count = cols.shape[0]
    tiles, parts, col_count, _ = own.shape
    seg_count = parts // 2
    row_count = 2 * col_count
    depth = 2 * LANES
    blk, group, blk_count = lax.axis_index("blk"), lax.axis_index("grp"), lax.axis_size("blk")
    step, half = pl.program_id(0), pl.program_id(1)

    def fetch(k, parity):
        source, index = picks[k][parity]
        array = rest[source] if index is None else rest[source].at[index]
        return pltpu.make_async_copy(array, cols.at[k], sems.at[k])

    @pl.when((step == 0) & (half == 0))
    def _():
        for parity in range(2):
            @pl.when(blk % 2 == parity)
            def _(parity=parity):
                for k in range(count):
                    fetch(k, parity).start()
        for source, place in ((own, group), (partner, 1 - group)):
            for q in range(tiles):
                rows[place, q] = source[q]

    for k in range(count):
        @pl.when((step == k) & (half == 0))
        def _(k=k):
            fetch(k, 0).wait()

    row_start = blk * row_count + half * col_count
    line = jnp.broadcast_to(ids[pl.ds(row_start // LANES, 1), :], (8, LANES))
    id_line = pltpu.roll(line, (LANES - row_start % LANES) % LANES, 1)[0:1, :]
    col_start = (blk + first + step) % blk_count * row_count + group * col_count
    for j in range(col_count):
        turn[j:j + 1, :] = jnp.where(id_line < info[col_start + j], 1.0, -1.0)

    lane = lax.broadcasted_iota(jnp.int32, (col_count, LANES), 1)
    low = lane <= TURN
    late = lane >= REST
    mirror = (TURN - lane) & (LANES - 1)

    def form(c, i, tile):
        b = i // PACK * PACK
        lines = [rows[half, tile, s, b:b + PACK, :] for s in range(parts)]
        r = [jnp.broadcast_to(v[i - b:i - b + 1, :], (col_count, LANES)) for v in lines]
        re = tree_sum([r[s] * c[s] for s in range(parts)])
        im = tree_sum([r[seg_count + s] * c[s] - r[s] * c[seg_count + s] for s in range(seg_count)])
        return re, im

    def push(h):
        deep = pl.ds(h * depth, depth)
        for unit, tab in enumerate((cos_tab, sin_tab)):
            side = jnp.concatenate([tab[0, deep, :], tab[1, deep, :]], axis=1)
            pltpu.matmul_push_rhs(side, staging_register=h % 2, mxu_index=unit)

    def finish(i, even, odd):
        sign = jnp.broadcast_to(turn[:, i:i + 1], (col_count, LANES))
        odd_u, odd_v = odd[:, :LANES] * sign, odd[:, LANES:] * sign
        even_u, even_v = even[:, :LANES], even[:, LANES:]
        ahead_u = (even_u + odd_u).astype(jnp.bfloat16)
        ahead_v = (even_v + odd_v).astype(jnp.bfloat16)
        back_u = jnp.take_along_axis(even_u - odd_u, mirror, axis=1, mode="promise_in_bounds")
        back_v = jnp.take_along_axis(even_v - odd_v, mirror, axis=1, mode="promise_in_bounds")
        line = out.at[0, 0, 0, i]
        line[:, 0:LANES] = back_u.astype(jnp.bfloat16)
        line[:, LANES:2 * LANES] = jnp.where(late, ahead_v, back_v.astype(jnp.bfloat16))
        line[:, 2 * LANES:3 * LANES] = jnp.where(low, ahead_v, ahead_u)
        line[:, 3 * LANES:] = ahead_u[:, :out.shape[-1] - 3 * LANES]

    def multiply(*sums):
        sums_even, sums_odd = sums[:col_count], sums[col_count:]
        push(0)
        for h in range(tiles // 2):
            if h + 1 < tiles // 2:
                push(h + 1)
            for g0 in range(0, col_count, TOGETHER):
                formed = []
                for tile in (2 * h, 2 * h + 1):
                    c = [cols[step, tile, s] for s in range(parts)]
                    formed.append([form(c, g0 + k, tile) for k in range(TOGETHER)])
                for k in range(TOGETHER):
                    g = g0 + k
                    fresh = h % 2 if g == 0 else None
                    for part, held in enumerate((sums_even, sums_odd)):
                        side = jnp.concatenate([formed[0][k][part], formed[1][k][part]], axis=1)
                        pltpu.matmul_acc_lhs(held[g], side, load_staged_rhs=fresh)
                    if h + 1 == tiles // 2 and g >= DELAY:
                        finish(g - DELAY, pltpu.matmul_pop(sums_even[g - DELAY]), pltpu.matmul_pop(sums_odd[g - DELAY]))
        for g in range(col_count - DELAY, col_count):
            finish(g, pltpu.matmul_pop(sums_even[g]), pltpu.matmul_pop(sums_odd[g]))

    pl.run_scoped(
        multiply,
        *[pltpu.ACC(0)((col_count, depth), jnp.float32)] * col_count,
        *[pltpu.ACC(1)((col_count, depth), jnp.float32)] * col_count,
    )

    if first == 0:
        @pl.when((step == 0) & (half == group))
        def _():
            for j in range(col_count):
                out[0, 0, 0, j, j:j + 1, :] = jnp.zeros((1, out.shape[-1]), jnp.bfloat16)


def correlate(info, plan_start, tables, own, partner, arrays, picks, first, output, step_count):
    count = len(picks)
    tiles, parts, col_count, _ = own.shape
    lag_count = 2 * HALF_LAG
    kept = [] if output is None else [output]
    ids = info.reshape(-1, LANES)

    def whole(array):
        return pl.BlockSpec(array.shape, lambda *_: (0,) * array.ndim)

    def slot(d, half, info):
        place = sum(jnp.where(info[plan_start + t] == first + d, t, 0) for t in range(step_count))
        return (0, place, 0, half, 0, 0)

    pairs = count * 2 * col_count * col_count * tiles * LANES
    return pl.pallas_call(
        functools.partial(correlate_kernel, first=first, picks=picks),
        grid_spec=pltpu.PrefetchScalarGridSpec(
            num_scalar_prefetch=1,
            grid=(count, 2),
            in_specs=[whole(ids), whole(tables[0]), whole(tables[1]), whole(own), whole(partner)]
            + [pl.BlockSpec(memory_space=pl.ANY)] * (len(arrays) + len(kept)),
            out_specs=pl.BlockSpec((1, 1, 1, col_count, col_count, lag_count), slot),
            scratch_shapes=[
                pltpu.VMEM((2, tiles, parts, col_count, LANES), jnp.bfloat16),
                pltpu.VMEM((col_count, LANES), jnp.float32),
                pltpu.VMEM((count, tiles, parts, col_count, LANES), jnp.bfloat16),
                pltpu.SemaphoreType.DMA((count,)),
            ],
        ),
        out_shape=jax.ShapeDtypeStruct((1, step_count, 1, 2 * col_count, col_count, lag_count), jnp.bfloat16),
        input_output_aliases={6 + len(arrays): 0} if kept else {},
        cost_estimate=pl.CostEstimate(flops=1600 * pairs, bytes_accessed=count * 3000000, transcendentals=0),
        compiler_params=pltpu.CompilerParams(vmem_limit_bytes=40 << 20),
    )(info, ids, *tables, own, partner, *arrays, *kept)


def whiten_tiles(spectra):
    whitened = whiten(spectra)
    channels, parts, freq_count = whitened.shape
    return jnp.transpose(whitened.reshape(channels, parts, freq_count // LANES, LANES), (2, 1, 0, 3))


def on_device_fused(spectra, channel_ids, plan):
    col_count, _, seg_count, freq_count = spectra.shape
    blk_count = lax.axis_size("blk")
    step_count = blk_count // 2 + 1
    id_count = channel_ids.shape[0]
    info = jnp.concatenate([channel_ids, plan[0], jnp.zeros((-(id_count + step_count) % (8 * LANES),), jnp.int32)])

    def other_core(block):
        return lax.ppermute(block, "blk", [(i ^ 1, i) for i in range(blk_count)])

    own = whiten_tiles(spectra)
    partner = passed_along(own, "grp", 1)
    sent, info = lax.optimization_barrier((own, info))
    near, far = passed_along(sent, "blk", -2), passed_along(sent, "blk", -4)
    tables = half_lag_tables(freq_count, 1.0 / math.sqrt(2.0 * freq_count * seg_count))

    def stage(arrays, picks, first, output):
        return correlate(info, id_count, tables, own, partner, arrays, picks, first, output, step_count)

    output = stage([own], [((0, None), (0, None))], 0, None)
    last = own
    for first in range(1, step_count, 4):
        if first == 1:
            near, far, last, output = lax.optimization_barrier((near, far, last, output))
            pair = jnp.stack([near, far])
            before = (other_core(last), None)
        else:
            pair, output = lax.optimization_barrier((later, output))
            before = (crossed, 1)
        if first + 4 < step_count:
            later = passed_along(pair, "blk", -4)
        crossed = other_core(pair)
        picks = [((0, before[1]), (2, 0)), ((1, 0),) * 2, ((2, 0), (2, 1)), ((1, 1),) * 2]
        output = stage([before[0], pair, crossed], picks, first, output)
    return output


def on_device(spectra, channel_ids, plan):
    col_count = spectra.shape[0]
    seg_count = spectra.shape[2]
    freq_count = spectra.shape[3]
    whitened = whiten(spectra)
    row_block = lax.all_gather(whitened, "grp", axis=0, tiled=True)
    row_count = row_block.shape[0]
    rotated = jnp.concatenate([row_block[:, seg_count:], -row_block[:, :seg_count]], axis=1)
    paired = jnp.stack([row_block, rotated])
    blk_count = lax.axis_size("blk")
    step_count = blk_count // 2 + 1
    blk_index = lax.axis_index("blk")
    grp_index = lax.axis_index("grp")
    cos_tab, sin_tab = lag_tables(freq_count)
    lag_count = cos_tab.shape[1]
    row_start = blk_index * row_count
    row_ids = lax.dynamic_slice_in_dim(channel_ids, row_start, row_count, 0)
    row_slots = row_start + jnp.arange(row_count, dtype=jnp.int32)
    slot_list = jnp.arange(step_count, dtype=jnp.int32)
    scaling = 1.0 / math.sqrt(2.0 * freq_count * seg_count)

    def correlate_one(offset, columns, output):
        col_start = (blk_index + offset) % blk_count * row_count + grp_index * col_count
        col_ids = lax.dynamic_slice_in_dim(channel_ids, col_start, col_count, 0)
        col_slots = col_start + jnp.arange(col_count, dtype=jnp.int32)
        cross_spec = jnp.einsum(
            "prsf,csf->prcf", paired, columns, preferred_element_type=jnp.float32
        )
        cross_spec = cross_spec.astype(jnp.bfloat16).reshape(2, row_count * col_count, freq_count)
        real_part = jnp.dot(cross_spec[0], cos_tab, preferred_element_type=jnp.float32)
        imag_part = jnp.dot(cross_spec[1], sin_tab, preferred_element_type=jnp.float32)
        orient = (
            jnp.where(row_ids[:, None] < col_ids[None, :], 1.0, -1.0)
            .astype(jnp.float32)
            .reshape(-1, 1)
        )
        keeper = (row_slots[:, None] != col_slots[None, :]).astype(jnp.float32).reshape(-1, 1)
        lagged = ((real_part + orient * imag_part) * (scaling * keeper)).astype(jnp.bfloat16)
        lagged = lagged.reshape(1, 1, 1, row_count, col_count, lag_count)
        out_slot = jnp.sum(slot_list * (plan[0] == offset).astype(jnp.int32))
        return lax.dynamic_update_slice(output, lagged, (0, out_slot, 0, 0, 0, 0))

    output = jnp.zeros((1, step_count, 1, row_count, col_count, lag_count), jnp.bfloat16)

    def advance(offset, carry):
        columns, output = carry
        output = correlate_one(offset, columns, output)
        columns = passed_along(columns, "blk", -1)
        return (columns, output)

    columns, output = lax.fori_loop(0, step_count - 1, advance, (whitened, output))
    output = correlate_one(step_count - 1, columns, output)
    return output


def solution(mesh):
    blk_count, grp_count = mesh.shape["blk"], mesh.shape["grp"]

    def program(spectra, channel_ids, plan):
        col_count = spectra.shape[0] // (blk_count * grp_count)
        fused = col_count == 2 * PACK and grp_count == 2 and blk_count % 8 == 0
        fused = fused and spectra.shape[3] % (4 * LANES) == 0
        return jax.shard_map(
            on_device_fused if fused else on_device,
            mesh=mesh,
            in_specs=(P(("blk", "grp"), None, None, None), P(), P("blk", None)),
            out_specs=P("blk", None, "grp", None, None, None),
            check_vma=False,
        )(spectra, channel_ids, plan)

    return program
```

```python
import functools
import math

import jax
import jax.numpy as jnp
from jax import lax
from jax.experimental import pallas as pl
from jax.experimental.pallas import tpu as pltpu
from jax.sharding import PartitionSpec as P

NFFT = 2000
HALF_LAG = 200
LANES = 128
PACK = 16
TURN = 16
REST = 72
MIDDLE = 56
TOGETHER = 8
DELAY = 2


def passed_along(block, axis, distance):
    devices = range(lax.axis_size(axis))
    route = [((i - distance) % len(devices), i) for i in devices]
    return lax.ppermute(block, axis, route)


def whiten(spectra):
    seg_power = jnp.mean(spectra * spectra, axis=(1, 3))
    whitened = spectra * lax.rsqrt(seg_power + 1e-06)[:, None, :, None]
    whitened = whitened.astype(jnp.bfloat16)
    return whitened.reshape(spectra.shape[0], 2 * spectra.shape[2], spectra.shape[3])


def lag_tables(freq_count):
    freq_axis = jnp.arange(freq_count, dtype=jnp.int32)
    lag_axis = jnp.arange(2 * HALF_LAG, dtype=jnp.int32) - HALF_LAG
    phase_index = freq_axis[:, None] * lag_axis[None, :] % NFFT
    angles = 2.0 * math.pi / NFFT * phase_index.astype(jnp.float32)
    weights = jnp.where(freq_axis == 0, 1.0, 2.0).astype(jnp.float32)[:, None]
    cos_tab = (weights * jnp.cos(angles)).astype(jnp.bfloat16)
    sin_tab = (-weights * jnp.sin(angles)).astype(jnp.bfloat16)
    return (cos_tab, sin_tab)


def tree_sum(terms):
    while len(terms) > 1:
        paired = [a + b for a, b in zip(terms[::2], terms[1::2])]
        terms = paired + terms[len(terms) - len(terms) % 2:]
    return terms[0]


def half_lag_tables(freq_count, scale):
    tile = lax.broadcasted_iota(jnp.int32, (2, 1, 1, LANES), 0)
    lane = lax.broadcasted_iota(jnp.int32, (2, 1, 1, LANES), 3)
    wrapped = jnp.where(lane <= TURN, MIDDLE + LANES + lane, MIDDLE + lane)
    lag = jnp.where(tile == 0, wrapped, jnp.where(lane <= TURN, MIDDLE + lane, jnp.maximum(lane - REST, 0)))
    coarse = PACK * jnp.arange(freq_count // PACK, dtype=jnp.int32)[None, :, None, None]
    fine = jnp.arange(PACK, dtype=jnp.int32)[None, None, :, None]

    def turned(freq):
        angles = 2.0 * math.pi / NFFT * (freq * lag % NFFT).astype(jnp.float32)
        return jnp.cos(angles), jnp.sin(angles)

    (cos_a, sin_a), (cos_b, sin_b) = lax.optimization_barrier((turned(coarse), turned(fine)))
    weights = jnp.where(coarse + fine == 0, scale, 2.0 * scale)
    cos_tab = (weights * (cos_a * cos_b - sin_a * sin_b)).astype(jnp.bfloat16)
    sin_tab = (-weights * (sin_a * cos_b + cos_a * sin_b)).astype(jnp.bfloat16)
    return cos_tab.reshape(2, freq_count, LANES), sin_tab.reshape(2, freq_count, LANES)


def correlate_kernel(info, ids, cos_tab, sin_tab, *rest, first, picks, side):
    sources, rest = rest[:2 - (side is not None)], rest[2 - (side is not None):]
    out, rows, turn, cols, sems = rest[-5:]
    count = cols.shape[0]
    tiles, parts, col_count, _ = sources[0].shape
    seg_count = parts // 2
    row_count = 2 * col_count
    depth = 2 * LANES
    blk, group, blk_count = lax.axis_index("blk"), lax.axis_index("grp"), lax.axis_size("blk")
    step = pl.program_id(0)
    half = pl.program_id(1) if side is None else (group + side) % 2
    opening = (step == 0) & (pl.program_id(1) == 0)

    def fetch(k, parity):
        source, index = picks[k][parity]
        array = rest[source] if index is None else rest[source].at[index]
        return pltpu.make_async_copy(array, cols.at[k], sems.at[k])

    @pl.when(opening)
    def _():
        for parity in range(2):
            @pl.when(blk % 2 == parity)
            def _(parity=parity):
                for k in range(count):
                    fetch(k, parity).start()
        for source, place in zip(sources, (group, 1 - group) if side is None else (half,)):
            for q in range(tiles):
                rows[place, q] = source[q]

    for k in range(count):
        @pl.when((step == k) & (pl.program_id(1) == 0))
        def _(k=k):
            fetch(k, 0).wait()

    row_start = blk * row_count + half * col_count
    line = jnp.broadcast_to(ids[pl.ds(row_start // LANES, 1), :], (8, LANES))
    id_line = pltpu.roll(line, (LANES - row_start % LANES) % LANES, 1)[0:1, :]
    col_start = (blk + first + step) % blk_count * row_count + group * col_count
    for j in range(col_count):
        turn[j:j + 1, :] = jnp.where(id_line < info[col_start + j], 1.0, -1.0)

    lane = lax.broadcasted_iota(jnp.int32, (col_count, LANES), 1)
    low = lane <= TURN
    late = lane >= REST
    mirror = (TURN - lane) & (LANES - 1)

    def form(c, i, tile):
        b = i // PACK * PACK
        lines = [rows[half, tile, s, b:b + PACK, :] for s in range(parts)]
        r = [jnp.broadcast_to(v[i - b:i - b + 1, :], (col_count, LANES)) for v in lines]
        re = tree_sum([r[s] * c[s] for s in range(parts)])
        im = tree_sum([r[seg_count + s] * c[s] - r[s] * c[seg_count + s] for s in range(seg_count)])
        return re, im

    def push(h):
        deep = pl.ds(h * depth, depth)
        for unit, tab in enumerate((cos_tab, sin_tab)):
            side = jnp.concatenate([tab[0, deep, :], tab[1, deep, :]], axis=1)
            pltpu.matmul_push_rhs(side, staging_register=h % 2, mxu_index=unit)

    def finish(i, even, odd):
        sign = jnp.broadcast_to(turn[:, i:i + 1], (col_count, LANES))
        odd_u, odd_v = odd[:, :LANES] * sign, odd[:, LANES:] * sign
        even_u, even_v = even[:, :LANES], even[:, LANES:]
        ahead_u = (even_u + odd_u).astype(jnp.bfloat16)
        ahead_v = (even_v + odd_v).astype(jnp.bfloat16)
        back_u = jnp.take_along_axis(even_u - odd_u, mirror, axis=1, mode="promise_in_bounds")
        back_v = jnp.take_along_axis(even_v - odd_v, mirror, axis=1, mode="promise_in_bounds")
        line = out.at[0, 0, 0, i]
        line[:, 0:LANES] = back_u.astype(jnp.bfloat16)
        line[:, LANES:2 * LANES] = jnp.where(late, ahead_v, back_v.astype(jnp.bfloat16))
        line[:, 2 * LANES:3 * LANES] = jnp.where(low, ahead_v, ahead_u)
        line[:, 3 * LANES:] = ahead_u[:, :out.shape[-1] - 3 * LANES]

    def multiply(*sums):
        sums_even, sums_odd = sums[:col_count], sums[col_count:]
        push(0)
        for h in range(tiles // 2):
            if h + 1 < tiles // 2:
                push(h + 1)
            for g0 in range(0, col_count, TOGETHER):
                formed = []
                for tile in (2 * h, 2 * h + 1):
                    c = [cols[step, tile, s] for s in range(parts)]
                    formed.append([form(c, g0 + k, tile) for k in range(TOGETHER)])
                for k in range(TOGETHER):
                    g = g0 + k
                    fresh = h % 2 if g == 0 else None
                    for part, held in enumerate((sums_even, sums_odd)):
                        side = jnp.concatenate([formed[0][k][part], formed[1][k][part]], axis=1)
                        pltpu.matmul_acc_lhs(held[g], side, load_staged_rhs=fresh)
                    if h + 1 == tiles // 2 and g >= DELAY:
                        finish(g - DELAY, pltpu.matmul_pop(sums_even[g - DELAY]), pltpu.matmul_pop(sums_odd[g - DELAY]))
        for g in range(col_count - DELAY, col_count):
            finish(g, pltpu.matmul_pop(sums_even[g]), pltpu.matmul_pop(sums_odd[g]))

    pl.run_scoped(
        multiply,
        *[pltpu.ACC(0)((col_count, depth), jnp.float32)] * col_count,
        *[pltpu.ACC(1)((col_count, depth), jnp.float32)] * col_count,
    )

    if first == 0 and side != 1:
        @pl.when((step == 0) & (half == group))
        def _():
            for j in range(col_count):
                out[0, 0, 0, j, j:j + 1, :] = jnp.zeros((1, out.shape[-1]), jnp.bfloat16)


def correlate(info, plan_start, tables, sources, arrays, picks, first, output, step_count, side):
    count = len(picks)
    tiles, parts, col_count, _ = sources[0].shape
    halves = 2 if side is None else 1
    lag_count = 2 * HALF_LAG
    kept = [] if output is None else [output]
    ids = info.reshape(-1, LANES)

    def whole(array):
        return pl.BlockSpec(array.shape, lambda *_: (0,) * array.ndim)

    def slot(d, half, info):
        place = sum(jnp.where(info[plan_start + t] == first + d, t, 0) for t in range(step_count))
        return (0, place, 0, half if side is None else (info[plan_start + step_count] + side) % 2, 0, 0)

    pairs = count * halves * col_count * col_count * tiles * LANES
    return pl.pallas_call(
        functools.partial(correlate_kernel, first=first, picks=picks, side=side),
        grid_spec=pltpu.PrefetchScalarGridSpec(
            num_scalar_prefetch=1,
            grid=(count, halves),
            in_specs=[whole(array) for array in (ids, *tables, *sources)]
            + [pl.BlockSpec(memory_space=pl.ANY)] * (len(arrays) + len(kept)),
            out_specs=pl.BlockSpec((1, 1, 1, col_count, col_count, lag_count), slot),
            scratch_shapes=[
                pltpu.VMEM((2, tiles, parts, col_count, LANES), jnp.bfloat16),
                pltpu.VMEM((col_count, LANES), jnp.float32),
                pltpu.VMEM((count, tiles, parts, col_count, LANES), jnp.bfloat16),
                pltpu.SemaphoreType.DMA((count,)),
            ],
        ),
        out_shape=jax.ShapeDtypeStruct((1, step_count, 1, 2 * col_count, col_count, lag_count), jnp.bfloat16),
        input_output_aliases={4 + len(sources) + len(arrays): 0} if kept else {},
        cost_estimate=pl.CostEstimate(flops=1600 * pairs, bytes_accessed=count * halves * 1500000, transcendentals=0),
        compiler_params=pltpu.CompilerParams(vmem_limit_bytes=40 << 20),
    )(info, ids, *tables, *sources, *arrays, *kept)


def whiten_tiles(spectra):
    whitened = whiten(spectra)
    channels, parts, freq_count = whitened.shape
    return jnp.transpose(whitened.reshape(channels, parts, freq_count // LANES, LANES), (2, 1, 0, 3))


def on_device_fused(spectra, channel_ids, plan):
    col_count, _, seg_count, freq_count = spectra.shape
    blk_count = lax.axis_size("blk")
    step_count = blk_count // 2 + 1
    id_count = channel_ids.shape[0]
    rest = jnp.zeros((-(id_count + step_count + 1) % (8 * LANES),), jnp.int32)
    info = jnp.concatenate([channel_ids, plan[0], lax.axis_index("grp")[None], rest])

    def other_core(block):
        return lax.ppermute(block, "blk", [(i ^ 1, i) for i in range(blk_count)])

    own = whiten_tiles(spectra)
    partner = passed_along(own, "grp", 1)
    sent, info = lax.optimization_barrier((own, info))
    near, far = passed_along(sent, "blk", -2), passed_along(sent, "blk", -4)
    tables = half_lag_tables(freq_count, 1.0 / math.sqrt(2.0 * freq_count * seg_count))

    def stage(sources, arrays, picks, first, output, side=None):
        return correlate(info, id_count, tables, sources, arrays, picks, first, output, step_count, side)

    alone = [((0, None), (0, None))]
    output = stage([own], [own], alone, 0, None, 0)
    last, partner, output = lax.optimization_barrier((own, partner, output))
    swapped = other_core(last)
    output = stage([partner], [own], alone, 0, output, 1)
    for first in range(1, step_count, 4):
        if first == 1:
            near, far, swapped, output = lax.optimization_barrier((near, far, swapped, output))
            pair = jnp.stack([near, far])
            before = (swapped, None)
        else:
            pair, output = lax.optimization_barrier((later, output))
            before = (crossed, 1)
        if first + 4 < step_count:
            later = passed_along(pair, "blk", -4)
        crossed = other_core(pair)
        picks = [((0, before[1]), (2, 0)), ((1, 0),) * 2, ((2, 0), (2, 1)), ((1, 1),) * 2]
        output = stage([own, partner], [before[0], pair, crossed], picks, first, output)
    return output


def on_device(spectra, channel_ids, plan):
    col_count = spectra.shape[0]
    seg_count = spectra.shape[2]
    freq_count = spectra.shape[3]
    whitened = whiten(spectra)
    row_block = lax.all_gather(whitened, "grp", axis=0, tiled=True)
    row_count = row_block.shape[0]
    rotated = jnp.concatenate([row_block[:, seg_count:], -row_block[:, :seg_count]], axis=1)
    paired = jnp.stack([row_block, rotated])
    blk_count = lax.axis_size("blk")
    step_count = blk_count // 2 + 1
    blk_index = lax.axis_index("blk")
    grp_index = lax.axis_index("grp")
    cos_tab, sin_tab = lag_tables(freq_count)
    lag_count = cos_tab.shape[1]
    row_start = blk_index * row_count
    row_ids = lax.dynamic_slice_in_dim(channel_ids, row_start, row_count, 0)
    row_slots = row_start + jnp.arange(row_count, dtype=jnp.int32)
    slot_list = jnp.arange(step_count, dtype=jnp.int32)
    scaling = 1.0 / math.sqrt(2.0 * freq_count * seg_count)

    def correlate_one(offset, columns, output):
        col_start = (blk_index + offset) % blk_count * row_count + grp_index * col_count
        col_ids = lax.dynamic_slice_in_dim(channel_ids, col_start, col_count, 0)
        col_slots = col_start + jnp.arange(col_count, dtype=jnp.int32)
        cross_spec = jnp.einsum(
            "prsf,csf->prcf", paired, columns, preferred_element_type=jnp.float32
        )
        cross_spec = cross_spec.astype(jnp.bfloat16).reshape(2, row_count * col_count, freq_count)
        real_part = jnp.dot(cross_spec[0], cos_tab, preferred_element_type=jnp.float32)
        imag_part = jnp.dot(cross_spec[1], sin_tab, preferred_element_type=jnp.float32)
        orient = (
            jnp.where(row_ids[:, None] < col_ids[None, :], 1.0, -1.0)
            .astype(jnp.float32)
            .reshape(-1, 1)
        )
        keeper = (row_slots[:, None] != col_slots[None, :]).astype(jnp.float32).reshape(-1, 1)
        lagged = ((real_part + orient * imag_part) * (scaling * keeper)).astype(jnp.bfloat16)
        lagged = lagged.reshape(1, 1, 1, row_count, col_count, lag_count)
        out_slot = jnp.sum(slot_list * (plan[0] == offset).astype(jnp.int32))
        return lax.dynamic_update_slice(output, lagged, (0, out_slot, 0, 0, 0, 0))

    output = jnp.zeros((1, step_count, 1, row_count, col_count, lag_count), jnp.bfloat16)

    def advance(offset, carry):
        columns, output = carry
        output = correlate_one(offset, columns, output)
        columns = passed_along(columns, "blk", -1)
        return (columns, output)

    columns, output = lax.fori_loop(0, step_count - 1, advance, (whitened, output))
    output = correlate_one(step_count - 1, columns, output)
    return output


def solution(mesh):
    blk_count, grp_count = mesh.shape["blk"], mesh.shape["grp"]

    def program(spectra, channel_ids, plan):
        col_count = spectra.shape[0] // (blk_count * grp_count)
        fused = col_count == 2 * PACK and grp_count == 2 and blk_count % 8 == 0
        fused = fused and spectra.shape[3] % (4 * LANES) == 0
        return jax.shard_map(
            on_device_fused if fused else on_device,
            mesh=mesh,
            in_specs=(P(("blk", "grp"), None, None, None), P(), P("blk", None)),
            out_specs=P("blk", None, "grp", None, None, None),
            check_vma=False,
        )(spectra, channel_ids, plan)

    return program
```

```python
import functools
import math

import jax
import jax.numpy as jnp
from jax import lax
from jax.experimental import pallas as pl
from jax.experimental.pallas import tpu as pltpu
from jax.sharding import PartitionSpec as P

NFFT = 2000
HALF_LAG = 200
LANES = 128
PACK = 16
TURN = 16
REST = 72
MIDDLE = 56
TOGETHER = 8
DELAY = 2


def passed_along(block, axis, distance):
    devices = range(lax.axis_size(axis))
    route = [((i - distance) % len(devices), i) for i in devices]
    return lax.ppermute(block, axis, route)


def whiten(spectra):
    seg_power = jnp.mean(spectra * spectra, axis=(1, 3))
    whitened = spectra * lax.rsqrt(seg_power + 1e-06)[:, None, :, None]
    whitened = whitened.astype(jnp.bfloat16)
    return whitened.reshape(spectra.shape[0], 2 * spectra.shape[2], spectra.shape[3])


def lag_tables(freq_count):
    freq_axis = jnp.arange(freq_count, dtype=jnp.int32)
    lag_axis = jnp.arange(2 * HALF_LAG, dtype=jnp.int32) - HALF_LAG
    phase_index = freq_axis[:, None] * lag_axis[None, :] % NFFT
    angles = 2.0 * math.pi / NFFT * phase_index.astype(jnp.float32)
    weights = jnp.where(freq_axis == 0, 1.0, 2.0).astype(jnp.float32)[:, None]
    cos_tab = (weights * jnp.cos(angles)).astype(jnp.bfloat16)
    sin_tab = (-weights * jnp.sin(angles)).astype(jnp.bfloat16)
    return (cos_tab, sin_tab)


def tree_sum(terms):
    while len(terms) > 1:
        paired = [a + b for a, b in zip(terms[::2], terms[1::2])]
        terms = paired + terms[len(terms) - len(terms) % 2:]
    return terms[0]


def half_lag_tables(freq_count, scale):
    tile = lax.broadcasted_iota(jnp.int32, (2, 1, 1, LANES), 0)
    lane = lax.broadcasted_iota(jnp.int32, (2, 1, 1, LANES), 3)
    wrapped = jnp.where(lane <= TURN, MIDDLE + LANES + lane, MIDDLE + lane)
    lag = jnp.where(tile == 0, wrapped, jnp.where(lane <= TURN, MIDDLE + lane, jnp.maximum(lane - REST, 0)))
    coarse = PACK * jnp.arange(freq_count // PACK, dtype=jnp.int32)[None, :, None, None]
    fine = jnp.arange(PACK, dtype=jnp.int32)[None, None, :, None]

    def turned(freq):
        angles = 2.0 * math.pi / NFFT * (freq * lag % NFFT).astype(jnp.float32)
        return jnp.cos(angles), jnp.sin(angles)

    (cos_a, sin_a), (cos_b, sin_b) = lax.optimization_barrier((turned(coarse), turned(fine)))
    weights = jnp.where(coarse + fine == 0, scale, 2.0 * scale)
    cos_tab = (weights * (cos_a * cos_b - sin_a * sin_b)).astype(jnp.bfloat16)
    sin_tab = (-weights * (sin_a * cos_b + cos_a * sin_b)).astype(jnp.bfloat16)
    return cos_tab.reshape(2, freq_count, LANES), sin_tab.reshape(2, freq_count, LANES)


def correlate_kernel(info, ids, cos_tab, sin_tab, *rest, first, picks, side):
    sources, rest = rest[:2 - (side is not None)], rest[2 - (side is not None):]
    out, rows, turn, cols, sems = rest[-5:]
    count = cols.shape[0]
    tiles, parts, col_count, _ = sources[0].shape
    seg_count = parts // 2
    row_count = 2 * col_count
    depth = 2 * LANES
    blk, group, blk_count = lax.axis_index("blk"), lax.axis_index("grp"), lax.axis_size("blk")
    step = pl.program_id(0)
    half = pl.program_id(1) if side is None else (group + side) % 2
    opening = (step == 0) & (pl.program_id(1) == 0)

    def fetch(k, parity):
        source, index = picks[k][parity]
        array = rest[source] if index is None else rest[source].at[index]
        return pltpu.make_async_copy(array, cols.at[k], sems.at[k])

    @pl.when(opening)
    def _():
        for parity in range(2):
            @pl.when(blk % 2 == parity)
            def _(parity=parity):
                for k in range(count):
                    fetch(k, parity).start()
        for source, place in zip(sources, (group, 1 - group) if side is None else (half,)):
            for q in range(tiles):
                rows[place, q] = source[q]

    for k in range(count):
        @pl.when((step == k) & (pl.program_id(1) == 0))
        def _(k=k):
            fetch(k, 0).wait()

    row_start = blk * row_count + half * col_count
    line = jnp.broadcast_to(ids[pl.ds(row_start // LANES, 1), :], (8, LANES))
    id_line = pltpu.roll(line, (LANES - row_start % LANES) % LANES, 1)[0:1, :]
    col_start = (blk + first + step) % blk_count * row_count + group * col_count
    for j in range(col_count):
        turn[j:j + 1, :] = jnp.where(id_line < info[col_start + j], 1.0, -1.0)

    lane = lax.broadcasted_iota(jnp.int32, (col_count, LANES), 1)
    low = lane <= TURN
    late = lane >= REST
    mirror = (TURN - lane) & (LANES - 1)

    def form(c, i, tile):
        b = i // PACK * PACK
        lines = [rows[half, tile, s, b:b + PACK, :] for s in range(parts)]
        r = [jnp.broadcast_to(v[i - b:i - b + 1, :], (col_count, LANES)) for v in lines]
        re = tree_sum([r[s] * c[s] for s in range(parts)])
        im = tree_sum([r[seg_count + s] * c[s] - r[s] * c[seg_count + s] for s in range(seg_count)])
        return re, im

    def push(h):
        deep = pl.ds(h * depth, depth)
        for unit, tab in enumerate((cos_tab, sin_tab)):
            side = jnp.concatenate([tab[0, deep, :], tab[1, deep, :]], axis=1)
            pltpu.matmul_push_rhs(side, staging_register=h % 2, mxu_index=unit)

    def finish(i, even, odd):
        sign = jnp.broadcast_to(turn[:, i:i + 1], (col_count, LANES))
        odd_u, odd_v = odd[:, :LANES] * sign, odd[:, LANES:] * sign
        even_u, even_v = even[:, :LANES], even[:, LANES:]
        ahead_u = (even_u + odd_u).astype(jnp.bfloat16)
        ahead_v = (even_v + odd_v).astype(jnp.bfloat16)
        back_u = jnp.take_along_axis(even_u - odd_u, mirror, axis=1, mode="promise_in_bounds")
        back_v = jnp.take_along_axis(even_v - odd_v, mirror, axis=1, mode="promise_in_bounds")
        line = out.at[0, 0, 0, i]
        line[:, 0:LANES] = back_u.astype(jnp.bfloat16)
        line[:, LANES:2 * LANES] = jnp.where(late, ahead_v, back_v.astype(jnp.bfloat16))
        line[:, 2 * LANES:3 * LANES] = jnp.where(low, ahead_v, ahead_u)
        line[:, 3 * LANES:] = ahead_u[:, :out.shape[-1] - 3 * LANES]

    def multiply(*sums):
        sums_even, sums_odd = sums[:col_count], sums[col_count:]
        push(0)
        for h in range(tiles // 2):
            if h + 1 < tiles // 2:
                push(h + 1)
            for g0 in range(0, col_count, TOGETHER):
                formed = []
                for tile in (2 * h, 2 * h + 1):
                    c = [cols[step, tile, s] for s in range(parts)]
                    formed.append([form(c, g0 + k, tile) for k in range(TOGETHER)])
                for k in range(TOGETHER):
                    g = g0 + k
                    fresh = h % 2 if g == 0 else None
                    for part, held in enumerate((sums_even, sums_odd)):
                        side = jnp.concatenate([formed[0][k][part], formed[1][k][part]], axis=1)
                        pltpu.matmul_acc_lhs(held[g], side, load_staged_rhs=fresh)
                    if h + 1 == tiles // 2 and g >= DELAY:
                        finish(g - DELAY, pltpu.matmul_pop(sums_even[g - DELAY]), pltpu.matmul_pop(sums_odd[g - DELAY]))
        for g in range(col_count - DELAY, col_count):
            finish(g, pltpu.matmul_pop(sums_even[g]), pltpu.matmul_pop(sums_odd[g]))

    pl.run_scoped(
        multiply,
        *[pltpu.ACC(0)((col_count, depth), jnp.float32)] * col_count,
        *[pltpu.ACC(1)((col_count, depth), jnp.float32)] * col_count,
    )

    if first == 0 and side != 1:
        @pl.when((step == 0) & (half == group))
        def _():
            for j in range(col_count):
                out[0, 0, 0, j, j:j + 1, :] = jnp.zeros((1, out.shape[-1]), jnp.bfloat16)


def correlate(info, plan_start, tables, sources, arrays, picks, first, output, step_count, side):
    count = len(picks)
    tiles, parts, col_count, _ = sources[0].shape
    halves = 2 if side is None else 1
    lag_count = 2 * HALF_LAG
    kept = [] if output is None else [output]
    ids = info.reshape(-1, LANES)

    def whole(array):
        return pl.BlockSpec(array.shape, lambda *_: (0,) * array.ndim)

    def slot(d, half, info):
        place = sum(jnp.where(info[plan_start + t] == first + d, t, 0) for t in range(step_count))
        return (0, place, 0, half if side is None else (info[plan_start + step_count] + side) % 2, 0, 0)

    pairs = count * halves * col_count * col_count * tiles * LANES
    return pl.pallas_call(
        functools.partial(correlate_kernel, first=first, picks=picks, side=side),
        grid_spec=pltpu.PrefetchScalarGridSpec(
            num_scalar_prefetch=1,
            grid=(count, halves),
            in_specs=[whole(array) for array in (ids, *tables, *sources)]
            + [pl.BlockSpec(memory_space=pl.ANY)] * (len(arrays) + len(kept)),
            out_specs=pl.BlockSpec((1, 1, 1, col_count, col_count, lag_count), slot),
            scratch_shapes=[
                pltpu.VMEM((2, tiles, parts, col_count, LANES), jnp.bfloat16),
                pltpu.VMEM((col_count, LANES), jnp.float32),
                pltpu.VMEM((count, tiles, parts, col_count, LANES), jnp.bfloat16),
                pltpu.SemaphoreType.DMA((count,)),
            ],
        ),
        out_shape=jax.ShapeDtypeStruct((1, step_count, 1, 2 * col_count, col_count, lag_count), jnp.bfloat16),
        input_output_aliases={4 + len(sources) + len(arrays): 0} if kept else {},
        cost_estimate=pl.CostEstimate(flops=1600 * pairs, bytes_accessed=count * halves * 1500000, transcendentals=0),
        compiler_params=pltpu.CompilerParams(vmem_limit_bytes=40 << 20),
    )(info, ids, *tables, *sources, *arrays, *kept)


def whiten_tiles(spectra):
    whitened = whiten(spectra)
    channels, parts, freq_count = whitened.shape
    return jnp.transpose(whitened.reshape(channels, parts, freq_count // LANES, LANES), (2, 1, 0, 3))


def on_device_fused(spectra, channel_ids, plan):
    col_count, _, seg_count, freq_count = spectra.shape
    blk_count = lax.axis_size("blk")
    step_count = blk_count // 2 + 1
    id_count = channel_ids.shape[0]
    rest = jnp.zeros((-(id_count + step_count + 1) % (8 * LANES),), jnp.int32)
    info = jnp.concatenate([channel_ids, plan[0], lax.axis_index("grp")[None], rest])

    def other_core(block):
        return lax.ppermute(block, "blk", [(i ^ 1, i) for i in range(blk_count)])

    own = whiten_tiles(spectra)
    partner = passed_along(own, "grp", 1)
    near, far = passed_along(own, "blk", -2), passed_along(own, "blk", -4)
    tables = half_lag_tables(freq_count, 1.0 / math.sqrt(2.0 * freq_count * seg_count))

    def stage(sources, arrays, picks, first, output, side=None):
        return correlate(info, id_count, tables, sources, arrays, picks, first, output, step_count, side)

    alone = [((0, None), (0, None))]
    output = stage([own], [own], alone, 0, None, 0)
    output = stage([partner], [own], alone, 0, output, 1)
    last, output = lax.optimization_barrier((own, output))
    swapped = other_core(last)
    for first in range(1, step_count, 4):
        if first == 1:
            near, far, swapped, output = lax.optimization_barrier((near, far, swapped, output))
            pair = jnp.stack([near, far])
            before = (swapped, None)
        else:
            pair, output = lax.optimization_barrier((later, output))
            before = (crossed, 1)
        if first + 4 < step_count:
            later = passed_along(pair, "blk", -4)
        crossed = other_core(pair)
        picks = [((0, before[1]), (2, 0)), ((1, 0),) * 2, ((2, 0), (2, 1)), ((1, 1),) * 2]
        output = stage([own, partner], [before[0], pair, crossed], picks, first, output)
    return output


def on_device(spectra, channel_ids, plan):
    col_count = spectra.shape[0]
    seg_count = spectra.shape[2]
    freq_count = spectra.shape[3]
    whitened = whiten(spectra)
    row_block = lax.all_gather(whitened, "grp", axis=0, tiled=True)
    row_count = row_block.shape[0]
    rotated = jnp.concatenate([row_block[:, seg_count:], -row_block[:, :seg_count]], axis=1)
    paired = jnp.stack([row_block, rotated])
    blk_count = lax.axis_size("blk")
    step_count = blk_count // 2 + 1
    blk_index = lax.axis_index("blk")
    grp_index = lax.axis_index("grp")
    cos_tab, sin_tab = lag_tables(freq_count)
    lag_count = cos_tab.shape[1]
    row_start = blk_index * row_count
    row_ids = lax.dynamic_slice_in_dim(channel_ids, row_start, row_count, 0)
    row_slots = row_start + jnp.arange(row_count, dtype=jnp.int32)
    slot_list = jnp.arange(step_count, dtype=jnp.int32)
    scaling = 1.0 / math.sqrt(2.0 * freq_count * seg_count)

    def correlate_one(offset, columns, output):
        col_start = (blk_index + offset) % blk_count * row_count + grp_index * col_count
        col_ids = lax.dynamic_slice_in_dim(channel_ids, col_start, col_count, 0)
        col_slots = col_start + jnp.arange(col_count, dtype=jnp.int32)
        cross_spec = jnp.einsum(
            "prsf,csf->prcf", paired, columns, preferred_element_type=jnp.float32
        )
        cross_spec = cross_spec.astype(jnp.bfloat16).reshape(2, row_count * col_count, freq_count)
        real_part = jnp.dot(cross_spec[0], cos_tab, preferred_element_type=jnp.float32)
        imag_part = jnp.dot(cross_spec[1], sin_tab, preferred_element_type=jnp.float32)
        orient = (
            jnp.where(row_ids[:, None] < col_ids[None, :], 1.0, -1.0)
            .astype(jnp.float32)
            .reshape(-1, 1)
        )
        keeper = (row_slots[:, None] != col_slots[None, :]).astype(jnp.float32).reshape(-1, 1)
        lagged = ((real_part + orient * imag_part) * (scaling * keeper)).astype(jnp.bfloat16)
        lagged = lagged.reshape(1, 1, 1, row_count, col_count, lag_count)
        out_slot = jnp.sum(slot_list * (plan[0] == offset).astype(jnp.int32))
        return lax.dynamic_update_slice(output, lagged, (0, out_slot, 0, 0, 0, 0))

    output = jnp.zeros((1, step_count, 1, row_count, col_count, lag_count), jnp.bfloat16)

    def advance(offset, carry):
        columns, output = carry
        output = correlate_one(offset, columns, output)
        columns = passed_along(columns, "blk", -1)
        return (columns, output)

    columns, output = lax.fori_loop(0, step_count - 1, advance, (whitened, output))
    output = correlate_one(step_count - 1, columns, output)
    return output


def solution(mesh):
    blk_count, grp_count = mesh.shape["blk"], mesh.shape["grp"]

    def program(spectra, channel_ids, plan):
        col_count = spectra.shape[0] // (blk_count * grp_count)
        fused = col_count == 2 * PACK and grp_count == 2 and blk_count % 8 == 0
        fused = fused and spectra.shape[3] % (4 * LANES) == 0
        return jax.shard_map(
            on_device_fused if fused else on_device,
            mesh=mesh,
            in_specs=(P(("blk", "grp"), None, None, None), P(), P("blk", None)),
            out_specs=P("blk", None, "grp", None, None, None),
            check_vma=False,
        )(spectra, channel_ids, plan)

    return program
```

```python
import functools
import math

import jax
import jax.numpy as jnp
from jax import lax
from jax.experimental import pallas as pl
from jax.experimental.pallas import tpu as pltpu
from jax.sharding import PartitionSpec as P

NFFT = 2000
HALF_LAG = 200
LANES = 128
PACK = 16
TURN = 16
REST = 72
MIDDLE = 56
TOGETHER = 8
DELAY = 2


def passed_along(block, axis, distance):
    devices = range(lax.axis_size(axis))
    route = [((i - distance) % len(devices), i) for i in devices]
    return lax.ppermute(block, axis, route)


def whiten(spectra):
    seg_power = jnp.mean(spectra * spectra, axis=(1, 3))
    whitened = spectra * lax.rsqrt(seg_power + 1e-06)[:, None, :, None]
    whitened = whitened.astype(jnp.bfloat16)
    return whitened.reshape(spectra.shape[0], 2 * spectra.shape[2], spectra.shape[3])


def lag_tables(freq_count):
    freq_axis = jnp.arange(freq_count, dtype=jnp.int32)
    lag_axis = jnp.arange(2 * HALF_LAG, dtype=jnp.int32) - HALF_LAG
    phase_index = freq_axis[:, None] * lag_axis[None, :] % NFFT
    angles = 2.0 * math.pi / NFFT * phase_index.astype(jnp.float32)
    weights = jnp.where(freq_axis == 0, 1.0, 2.0).astype(jnp.float32)[:, None]
    cos_tab = (weights * jnp.cos(angles)).astype(jnp.bfloat16)
    sin_tab = (-weights * jnp.sin(angles)).astype(jnp.bfloat16)
    return (cos_tab, sin_tab)


def tree_sum(terms):
    while len(terms) > 1:
        paired = [a + b for a, b in zip(terms[::2], terms[1::2])]
        terms = paired + terms[len(terms) - len(terms) % 2:]
    return terms[0]


def half_lag_tables(freq_count, scale):
    tile = lax.broadcasted_iota(jnp.int32, (2, 1, 1, LANES), 0)
    lane = lax.broadcasted_iota(jnp.int32, (2, 1, 1, LANES), 3)
    wrapped = jnp.where(lane <= TURN, MIDDLE + LANES + lane, MIDDLE + lane)
    lag = jnp.where(tile == 0, wrapped, jnp.where(lane <= TURN, MIDDLE + lane, jnp.maximum(lane - REST, 0)))
    coarse = PACK * jnp.arange(freq_count // PACK, dtype=jnp.int32)[None, :, None, None]
    fine = jnp.arange(PACK, dtype=jnp.int32)[None, None, :, None]

    def turned(freq):
        angles = 2.0 * math.pi / NFFT * (freq * lag % NFFT).astype(jnp.float32)
        return jnp.cos(angles), jnp.sin(angles)

    (cos_a, sin_a), (cos_b, sin_b) = lax.optimization_barrier((turned(coarse), turned(fine)))
    weights = jnp.where(coarse + fine == 0, scale, 2.0 * scale)
    cos_tab = (weights * (cos_a * cos_b - sin_a * sin_b)).astype(jnp.bfloat16)
    sin_tab = (-weights * (sin_a * cos_b + cos_a * sin_b)).astype(jnp.bfloat16)
    return cos_tab.reshape(2, freq_count, LANES), sin_tab.reshape(2, freq_count, LANES)


def correlate_kernel(info, ids, cos_tab, sin_tab, *rest, first, picks, side):
    sources, rest = rest[:2 - (side is not None)], rest[2 - (side is not None):]
    out, rows, turn, cols, sems = rest[-5:]
    count = cols.shape[0]
    tiles, parts, col_count, _ = sources[0].shape
    seg_count = parts // 2
    row_count = 2 * col_count
    depth = 2 * LANES
    blk, group, blk_count = lax.axis_index("blk"), lax.axis_index("grp"), lax.axis_size("blk")
    step = pl.program_id(0)
    half = pl.program_id(1) if side is None else (group + side) % 2
    opening = (step == 0) & (pl.program_id(1) == 0)

    def fetch(k, parity):
        source, index = picks[k][parity]
        array = rest[source] if index is None else rest[source].at[index]
        return pltpu.make_async_copy(array, cols.at[k], sems.at[k])

    @pl.when(opening)
    def _():
        for parity in range(2):
            @pl.when(blk % 2 == parity)
            def _(parity=parity):
                for k in range(count):
                    fetch(k, parity).start()
        for source, place in zip(sources, (group, 1 - group) if side is None else (half,)):
            for q in range(tiles):
                rows[place, q] = source[q]

    for k in range(count):
        @pl.when((step == k) & (pl.program_id(1) == 0))
        def _(k=k):
            fetch(k, 0).wait()

    row_start = blk * row_count + half * col_count
    line = jnp.broadcast_to(ids[pl.ds(row_start // LANES, 1), :], (8, LANES))
    id_line = pltpu.roll(line, (LANES - row_start % LANES) % LANES, 1)[0:1, :]
    col_start = (blk + first + step) % blk_count * row_count + group * col_count
    for j in range(col_count):
        turn[j:j + 1, :] = jnp.where(id_line < info[col_start + j], 1.0, -1.0)

    lane = lax.broadcasted_iota(jnp.int32, (col_count, LANES), 1)
    low = lane <= TURN
    late = lane >= REST
    mirror = (TURN - lane) & (LANES - 1)

    def form(c, i, tile):
        b = i // PACK * PACK
        lines = [rows[half, tile, s, b:b + PACK, :] for s in range(parts)]
        r = [jnp.broadcast_to(v[i - b:i - b + 1, :], (col_count, LANES)) for v in lines]
        re = tree_sum([r[s] * c[s] for s in range(parts)])
        im = tree_sum([r[seg_count + s] * c[s] - r[s] * c[seg_count + s] for s in range(seg_count)])
        return re, im

    def push(h):
        deep = pl.ds(h * depth, depth)
        for unit, tab in enumerate((cos_tab, sin_tab)):
            side = jnp.concatenate([tab[0, deep, :], tab[1, deep, :]], axis=1)
            pltpu.matmul_push_rhs(side, staging_register=h % 2, mxu_index=unit)

    def finish(i, even, odd):
        sign = jnp.broadcast_to(turn[:, i:i + 1], (col_count, LANES))
        odd_u, odd_v = odd[:, :LANES] * sign, odd[:, LANES:] * sign
        even_u, even_v = even[:, :LANES], even[:, LANES:]
        ahead_u = (even_u + odd_u).astype(jnp.bfloat16)
        ahead_v = (even_v + odd_v).astype(jnp.bfloat16)
        back_u = jnp.take_along_axis(even_u - odd_u, mirror, axis=1, mode="promise_in_bounds")
        back_v = jnp.take_along_axis(even_v - odd_v, mirror, axis=1, mode="promise_in_bounds")
        line = out.at[0, 0, 0, i]
        line[:, 0:LANES] = back_u.astype(jnp.bfloat16)
        line[:, LANES:2 * LANES] = jnp.where(late, ahead_v, back_v.astype(jnp.bfloat16))
        line[:, 2 * LANES:3 * LANES] = jnp.where(low, ahead_v, ahead_u)
        line[:, 3 * LANES:] = ahead_u[:, :out.shape[-1] - 3 * LANES]

    def multiply(*sums):
        sums_even, sums_odd = sums[:col_count], sums[col_count:]
        push(0)
        for h in range(tiles // 2):
            if h + 1 < tiles // 2:
                push(h + 1)
            for g0 in range(0, col_count, TOGETHER):
                formed = []
                for tile in (2 * h, 2 * h + 1):
                    c = [cols[step, tile, s] for s in range(parts)]
                    formed.append([form(c, g0 + k, tile) for k in range(TOGETHER)])
                for k in range(TOGETHER):
                    g = g0 + k
                    fresh = h % 2 if g == 0 else None
                    for part, held in enumerate((sums_even, sums_odd)):
                        side = jnp.concatenate([formed[0][k][part], formed[1][k][part]], axis=1)
                        pltpu.matmul_acc_lhs(held[g], side, load_staged_rhs=fresh)
                    if h + 1 == tiles // 2 and g >= DELAY:
                        finish(g - DELAY, pltpu.matmul_pop(sums_even[g - DELAY]), pltpu.matmul_pop(sums_odd[g - DELAY]))
        for g in range(col_count - DELAY, col_count):
            finish(g, pltpu.matmul_pop(sums_even[g]), pltpu.matmul_pop(sums_odd[g]))

    pl.run_scoped(
        multiply,
        *[pltpu.ACC(0)((col_count, depth), jnp.float32)] * col_count,
        *[pltpu.ACC(1)((col_count, depth), jnp.float32)] * col_count,
    )

    if first == 0 and side != 1:
        @pl.when((step == 0) & (half == group))
        def _():
            for j in range(col_count):
                out[0, 0, 0, j, j:j + 1, :] = jnp.zeros((1, out.shape[-1]), jnp.bfloat16)


def correlate(info, plan_start, tables, sources, arrays, picks, first, output, step_count, side):
    count = len(picks)
    tiles, parts, col_count, _ = sources[0].shape
    halves = 2 if side is None else 1
    lag_count = 2 * HALF_LAG
    kept = [] if output is None else [output]
    ids = info.reshape(-1, LANES)

    def whole(array):
        return pl.BlockSpec(array.shape, lambda *_: (0,) * array.ndim)

    def slot(d, half, info):
        place = sum(jnp.where(info[plan_start + t] == first + d, t, 0) for t in range(step_count))
        return (0, place, 0, half if side is None else (info[plan_start + step_count] + side) % 2, 0, 0)

    pairs = count * halves * col_count * col_count * tiles * LANES
    return pl.pallas_call(
        functools.partial(correlate_kernel, first=first, picks=picks, side=side),
        grid_spec=pltpu.PrefetchScalarGridSpec(
            num_scalar_prefetch=1,
            grid=(count, halves),
            in_specs=[whole(array) for array in (ids, *tables, *sources)]
            + [pl.BlockSpec(memory_space=pl.ANY)] * (len(arrays) + len(kept)),
            out_specs=pl.BlockSpec((1, 1, 1, col_count, col_count, lag_count), slot),
            scratch_shapes=[
                pltpu.VMEM((2, tiles, parts, col_count, LANES), jnp.bfloat16),
                pltpu.VMEM((col_count, LANES), jnp.float32),
                pltpu.VMEM((count, tiles, parts, col_count, LANES), jnp.bfloat16),
                pltpu.SemaphoreType.DMA((count,)),
            ],
        ),
        out_shape=jax.ShapeDtypeStruct((1, step_count, 1, 2 * col_count, col_count, lag_count), jnp.bfloat16),
        input_output_aliases={4 + len(sources) + len(arrays): 0} if kept else {},
        cost_estimate=pl.CostEstimate(flops=1600 * pairs, bytes_accessed=count * halves * 1500000, transcendentals=0),
        compiler_params=pltpu.CompilerParams(vmem_limit_bytes=40 << 20),
    )(info, ids, *tables, *sources, *arrays, *kept)


def whiten_kernel(spectra, out):
    channels, halves, seg_count, freq_count = spectra.shape
    for s in range(seg_count):
        lines = [spectra[:, p, s, :] for p in range(halves)]
        power = sum(jnp.sum(line * line, axis=1, keepdims=True) for line in lines)
        level = lax.rsqrt(power / (halves * freq_count) + 1e-06)
        for p, line in enumerate(lines):
            for q in range(freq_count // LANES):
                tile = line[:, q * LANES:(q + 1) * LANES] * level
                out[q, p * seg_count + s] = tile.astype(jnp.bfloat16)


def whiten_tiles(spectra):
    channels, halves, seg_count, freq_count = spectra.shape
    shape = (freq_count // LANES, halves * seg_count, channels, LANES)
    return pl.pallas_call(whiten_kernel, out_shape=jax.ShapeDtypeStruct(shape, jnp.bfloat16))(spectra)


def on_device_fused(spectra, channel_ids, plan):
    col_count, _, seg_count, freq_count = spectra.shape
    blk_count = lax.axis_size("blk")
    step_count = blk_count // 2 + 1
    id_count = channel_ids.shape[0]
    rest = jnp.zeros((-(id_count + step_count + 1) % (8 * LANES),), jnp.int32)
    info = jnp.concatenate([channel_ids, plan[0], lax.axis_index("grp")[None], rest])

    def other_core(block):
        return lax.ppermute(block, "blk", [(i ^ 1, i) for i in range(blk_count)])

    own = whiten_tiles(spectra)
    partner = passed_along(own, "grp", 1)
    near, far = passed_along(own, "blk", -2), passed_along(own, "blk", -4)
    tables = half_lag_tables(freq_count, 1.0 / math.sqrt(2.0 * freq_count * seg_count))

    def stage(sources, arrays, picks, first, output, side=None):
        return correlate(info, id_count, tables, sources, arrays, picks, first, output, step_count, side)

    alone = [((0, None), (0, None))]
    output = stage([own], [own], alone, 0, None, 0)
    output = stage([partner], [own], alone, 0, output, 1)
    last, output = lax.optimization_barrier((own, output))
    swapped = other_core(last)
    for first in range(1, step_count, 4):
        if first == 1:
            near, far, swapped, output = lax.optimization_barrier((near, far, swapped, output))
            pair = jnp.stack([near, far])
            before = (swapped, None)
        else:
            pair, output = lax.optimization_barrier((later, output))
            before = (crossed, 1)
        if first + 4 < step_count:
            later = passed_along(pair, "blk", -4)
        crossed = other_core(pair)
        picks = [((0, before[1]), (2, 0)), ((1, 0),) * 2, ((2, 0), (2, 1)), ((1, 1),) * 2]
        output = stage([own, partner], [before[0], pair, crossed], picks, first, output)
    return output


def on_device(spectra, channel_ids, plan):
    col_count = spectra.shape[0]
    seg_count = spectra.shape[2]
    freq_count = spectra.shape[3]
    whitened = whiten(spectra)
    row_block = lax.all_gather(whitened, "grp", axis=0, tiled=True)
    row_count = row_block.shape[0]
    rotated = jnp.concatenate([row_block[:, seg_count:], -row_block[:, :seg_count]], axis=1)
    paired = jnp.stack([row_block, rotated])
    blk_count = lax.axis_size("blk")
    step_count = blk_count // 2 + 1
    blk_index = lax.axis_index("blk")
    grp_index = lax.axis_index("grp")
    cos_tab, sin_tab = lag_tables(freq_count)
    lag_count = cos_tab.shape[1]
    row_start = blk_index * row_count
    row_ids = lax.dynamic_slice_in_dim(channel_ids, row_start, row_count, 0)
    row_slots = row_start + jnp.arange(row_count, dtype=jnp.int32)
    slot_list = jnp.arange(step_count, dtype=jnp.int32)
    scaling = 1.0 / math.sqrt(2.0 * freq_count * seg_count)

    def correlate_one(offset, columns, output):
        col_start = (blk_index + offset) % blk_count * row_count + grp_index * col_count
        col_ids = lax.dynamic_slice_in_dim(channel_ids, col_start, col_count, 0)
        col_slots = col_start + jnp.arange(col_count, dtype=jnp.int32)
        cross_spec = jnp.einsum(
            "prsf,csf->prcf", paired, columns, preferred_element_type=jnp.float32
        )
        cross_spec = cross_spec.astype(jnp.bfloat16).reshape(2, row_count * col_count, freq_count)
        real_part = jnp.dot(cross_spec[0], cos_tab, preferred_element_type=jnp.float32)
        imag_part = jnp.dot(cross_spec[1], sin_tab, preferred_element_type=jnp.float32)
        orient = (
            jnp.where(row_ids[:, None] < col_ids[None, :], 1.0, -1.0)
            .astype(jnp.float32)
            .reshape(-1, 1)
        )
        keeper = (row_slots[:, None] != col_slots[None, :]).astype(jnp.float32).reshape(-1, 1)
        lagged = ((real_part + orient * imag_part) * (scaling * keeper)).astype(jnp.bfloat16)
        lagged = lagged.reshape(1, 1, 1, row_count, col_count, lag_count)
        out_slot = jnp.sum(slot_list * (plan[0] == offset).astype(jnp.int32))
        return lax.dynamic_update_slice(output, lagged, (0, out_slot, 0, 0, 0, 0))

    output = jnp.zeros((1, step_count, 1, row_count, col_count, lag_count), jnp.bfloat16)

    def advance(offset, carry):
        columns, output = carry
        output = correlate_one(offset, columns, output)
        columns = passed_along(columns, "blk", -1)
        return (columns, output)

    columns, output = lax.fori_loop(0, step_count - 1, advance, (whitened, output))
    output = correlate_one(step_count - 1, columns, output)
    return output


def solution(mesh):
    blk_count, grp_count = mesh.shape["blk"], mesh.shape["grp"]

    def program(spectra, channel_ids, plan):
        col_count = spectra.shape[0] // (blk_count * grp_count)
        fused = col_count == 2 * PACK and grp_count == 2 and blk_count % 8 == 0
        fused = fused and spectra.shape[3] % (4 * LANES) == 0
        return jax.shard_map(
            on_device_fused if fused else on_device,
            mesh=mesh,
            in_specs=(P(("blk", "grp"), None, None, None), P(), P("blk", None)),
            out_specs=P("blk", None, "grp", None, None, None),
            check_vma=False,
        )(spectra, channel_ids, plan)

    return program
```

```python
import functools
import math

import jax
import jax.numpy as jnp
from jax import lax
from jax.experimental import pallas as pl
from jax.experimental.pallas import tpu as pltpu
from jax.sharding import PartitionSpec as P

NFFT = 2000
HALF_LAG = 200
LANES = 128
PACK = 16
TURN = 16
REST = 72
MIDDLE = 56
TOGETHER = 8
DELAY = 2


def passed_along(block, axis, distance):
    devices = range(lax.axis_size(axis))
    route = [((i - distance) % len(devices), i) for i in devices]
    return lax.ppermute(block, axis, route)


def whiten(spectra):
    seg_power = jnp.mean(spectra * spectra, axis=(1, 3))
    whitened = spectra * lax.rsqrt(seg_power + 1e-06)[:, None, :, None]
    whitened = whitened.astype(jnp.bfloat16)
    return whitened.reshape(spectra.shape[0], 2 * spectra.shape[2], spectra.shape[3])


def lag_tables(freq_count):
    freq_axis = jnp.arange(freq_count, dtype=jnp.int32)
    lag_axis = jnp.arange(2 * HALF_LAG, dtype=jnp.int32) - HALF_LAG
    phase_index = freq_axis[:, None] * lag_axis[None, :] % NFFT
    angles = 2.0 * math.pi / NFFT * phase_index.astype(jnp.float32)
    weights = jnp.where(freq_axis == 0, 1.0, 2.0).astype(jnp.float32)[:, None]
    cos_tab = (weights * jnp.cos(angles)).astype(jnp.bfloat16)
    sin_tab = (-weights * jnp.sin(angles)).astype(jnp.bfloat16)
    return (cos_tab, sin_tab)


def tree_sum(terms):
    while len(terms) > 1:
        paired = [a + b for a, b in zip(terms[::2], terms[1::2])]
        terms = paired + terms[len(terms) - len(terms) % 2:]
    return terms[0]


def half_lag_tables(freq_count, scale):
    tile = lax.broadcasted_iota(jnp.int32, (2, 1, 1, LANES), 0)
    lane = lax.broadcasted_iota(jnp.int32, (2, 1, 1, LANES), 3)
    wrapped = jnp.where(lane <= TURN, MIDDLE + LANES + lane, MIDDLE + lane)
    lag = jnp.where(tile == 0, wrapped, jnp.where(lane <= TURN, MIDDLE + lane, jnp.maximum(lane - REST, 0)))
    coarse = PACK * jnp.arange(freq_count // PACK, dtype=jnp.int32)[None, :, None, None]
    fine = jnp.arange(PACK, dtype=jnp.int32)[None, None, :, None]

    def turned(freq):
        angles = 2.0 * math.pi / NFFT * (freq * lag % NFFT).astype(jnp.float32)
        return jnp.cos(angles), jnp.sin(angles)

    (cos_a, sin_a), (cos_b, sin_b) = lax.optimization_barrier((turned(coarse), turned(fine)))
    weights = jnp.where(coarse + fine == 0, scale, 2.0 * scale)
    cos_tab = (weights * (cos_a * cos_b - sin_a * sin_b)).astype(jnp.bfloat16)
    sin_tab = (-weights * (sin_a * cos_b + cos_a * sin_b)).astype(jnp.bfloat16)
    return cos_tab.reshape(2, freq_count, LANES), sin_tab.reshape(2, freq_count, LANES)


def correlate_kernel(info, ids, cos_tab, sin_tab, *rest, first, picks, side):
    sources, rest = rest[:2 - (side is not None)], rest[2 - (side is not None):]
    out, rows, turn, cols, sems = rest[-5:]
    count = cols.shape[0]
    tiles, parts, col_count, _ = sources[0].shape
    seg_count = parts // 2
    row_count = 2 * col_count
    depth = 2 * LANES
    blk, group, blk_count = lax.axis_index("blk"), lax.axis_index("grp"), lax.axis_size("blk")
    step = pl.program_id(0)
    half = pl.program_id(1) if side is None else (group + side) % 2
    opening = (step == 0) & (pl.program_id(1) == 0)

    def fetch(k, parity):
        source, index = picks[k][parity]
        array = rest[source] if index is None else rest[source].at[index]
        return pltpu.make_async_copy(array, cols.at[k], sems.at[k])

    @pl.when(opening)
    def _():
        for parity in range(2):
            @pl.when(blk % 2 == parity)
            def _(parity=parity):
                for k in range(count):
                    fetch(k, parity).start()
        for source, place in zip(sources, (group, 1 - group) if side is None else (half,)):
            for q in range(tiles):
                rows[place, q] = source[q]

    for k in range(count):
        @pl.when((step == k) & (pl.program_id(1) == 0))
        def _(k=k):
            fetch(k, 0).wait()

    row_start = blk * row_count + half * col_count
    line = jnp.broadcast_to(ids[pl.ds(row_start // LANES, 1), :], (8, LANES))
    id_line = pltpu.roll(line, (LANES - row_start % LANES) % LANES, 1)[0:1, :]
    col_start = (blk + first + step) % blk_count * row_count + group * col_count
    for j in range(col_count):
        turn[j:j + 1, :] = jnp.where(id_line < info[col_start + j], 1.0, -1.0)

    lane = lax.broadcasted_iota(jnp.int32, (col_count, LANES), 1)
    low = lane <= TURN
    late = lane >= REST
    mirror = (TURN - lane) & (LANES - 1)

    def form(c, i, tile):
        b = i // PACK * PACK
        lines = [rows[half, tile, s, b:b + PACK, :] for s in range(parts)]
        r = [jnp.broadcast_to(v[i - b:i - b + 1, :], (col_count, LANES)) for v in lines]
        re = tree_sum([r[s] * c[s] for s in range(parts)])
        im = tree_sum([r[seg_count + s] * c[s] - r[s] * c[seg_count + s] for s in range(seg_count)])
        return re, im

    def push(h):
        deep = pl.ds(h * depth, depth)
        for unit, tab in enumerate((cos_tab, sin_tab)):
            side = jnp.concatenate([tab[0, deep, :], tab[1, deep, :]], axis=1)
            pltpu.matmul_push_rhs(side, staging_register=h % 2, mxu_index=unit)

    def finish(i, even, odd):
        sign = jnp.broadcast_to(turn[:, i:i + 1], (col_count, LANES))
        odd_u, odd_v = odd[:, :LANES] * sign, odd[:, LANES:] * sign
        even_u, even_v = even[:, :LANES], even[:, LANES:]
        ahead_u = (even_u + odd_u).astype(jnp.bfloat16)
        ahead_v = (even_v + odd_v).astype(jnp.bfloat16)
        back_u = jnp.take_along_axis(even_u - odd_u, mirror, axis=1, mode="promise_in_bounds")
        back_v = jnp.take_along_axis(even_v - odd_v, mirror, axis=1, mode="promise_in_bounds")
        line = out.at[0, 0, 0, i]
        line[:, 0:LANES] = back_u.astype(jnp.bfloat16)
        line[:, LANES:2 * LANES] = jnp.where(late, ahead_v, back_v.astype(jnp.bfloat16))
        line[:, 2 * LANES:3 * LANES] = jnp.where(low, ahead_v, ahead_u)
        line[:, 3 * LANES:] = ahead_u[:, :out.shape[-1] - 3 * LANES]

    def multiply(*sums):
        sums_even, sums_odd = sums[:col_count], sums[col_count:]
        push(0)
        for h in range(tiles // 2):
            if h + 1 < tiles // 2:
                push(h + 1)
            for g0 in range(0, col_count, TOGETHER):
                formed = []
                for tile in (2 * h, 2 * h + 1):
                    c = [cols[step, tile, s] for s in range(parts)]
                    formed.append([form(c, g0 + k, tile) for k in range(TOGETHER)])
                for k in range(TOGETHER):
                    g = g0 + k
                    fresh = h % 2 if g == 0 else None
                    for part, held in enumerate((sums_even, sums_odd)):
                        side = jnp.concatenate([formed[0][k][part], formed[1][k][part]], axis=1)
                        pltpu.matmul_acc_lhs(held[g], side, load_staged_rhs=fresh)
                    if h + 1 == tiles // 2 and g >= DELAY:
                        finish(g - DELAY, pltpu.matmul_pop(sums_even[g - DELAY]), pltpu.matmul_pop(sums_odd[g - DELAY]))
        for g in range(col_count - DELAY, col_count):
            finish(g, pltpu.matmul_pop(sums_even[g]), pltpu.matmul_pop(sums_odd[g]))

    pl.run_scoped(
        multiply,
        *[pltpu.ACC(0)((col_count, depth), jnp.float32)] * col_count,
        *[pltpu.ACC(1)((col_count, depth), jnp.float32)] * col_count,
    )

    if first == 0 and side != 1:
        @pl.when((step == 0) & (half == group))
        def _():
            for j in range(col_count):
                out[0, 0, 0, j, j:j + 1, :] = jnp.zeros((1, out.shape[-1]), jnp.bfloat16)


def correlate(info, plan_start, tables, sources, arrays, picks, first, output, step_count, side):
    count = len(picks)
    tiles, parts, col_count, _ = sources[0].shape
    halves = 2 if side is None else 1
    lag_count = 2 * HALF_LAG
    kept = [] if output is None else [output]
    ids = info.reshape(-1, LANES)

    def whole(array):
        return pl.BlockSpec(array.shape, lambda *_: (0,) * array.ndim)

    def slot(d, half, info):
        place = sum(jnp.where(info[plan_start + t] == first + d, t, 0) for t in range(step_count))
        return (0, place, 0, half if side is None else (info[plan_start + step_count] + side) % 2, 0, 0)

    pairs = count * halves * col_count * col_count * tiles * LANES
    return pl.pallas_call(
        functools.partial(correlate_kernel, first=first, picks=picks, side=side),
        grid_spec=pltpu.PrefetchScalarGridSpec(
            num_scalar_prefetch=1,
            grid=(count, halves),
            in_specs=[whole(array) for array in (ids, *tables, *sources)]
            + [pl.BlockSpec(memory_space=pl.ANY)] * (len(arrays) + len(kept)),
            out_specs=pl.BlockSpec((1, 1, 1, col_count, col_count, lag_count), slot),
            scratch_shapes=[
                pltpu.VMEM((2, tiles, parts, col_count, LANES), jnp.bfloat16),
                pltpu.VMEM((col_count, LANES), jnp.float32),
                pltpu.VMEM((count, tiles, parts, col_count, LANES), jnp.bfloat16),
                pltpu.SemaphoreType.DMA((count,)),
            ],
        ),
        out_shape=jax.ShapeDtypeStruct((1, step_count, 1, 2 * col_count, col_count, lag_count), jnp.bfloat16),
        input_output_aliases={4 + len(sources) + len(arrays): 0} if kept else {},
        cost_estimate=pl.CostEstimate(flops=1600 * pairs, bytes_accessed=count * halves * 1500000, transcendentals=0),
        compiler_params=pltpu.CompilerParams(vmem_limit_bytes=40 << 20),
    )(info, ids, *tables, *sources, *arrays, *kept)


def whiten_kernel(spectra, out):
    channels, halves, seg_count, freq_count = spectra.shape
    for s in range(seg_count):
        lines = [spectra[:, p, s, :] for p in range(halves)]
        power = sum(jnp.sum(line * line, axis=1, keepdims=True) for line in lines)
        level = lax.rsqrt(power / (halves * freq_count) + 1e-06)
        for p, line in enumerate(lines):
            for q in range(freq_count // LANES):
                tile = line[:, q * LANES:(q + 1) * LANES] * level
                out[q, p * seg_count + s] = tile.astype(jnp.bfloat16)


def whiten_tiles(spectra):
    channels, halves, seg_count, freq_count = spectra.shape
    shape = (freq_count // LANES, halves * seg_count, channels, LANES)
    return pl.pallas_call(
        whiten_kernel,
        out_specs=pl.BlockSpec(memory_space=pltpu.VMEM),
        out_shape=pltpu.VMEM(shape, jnp.bfloat16),
    )(spectra)


def on_device_fused(spectra, channel_ids, plan):
    col_count, _, seg_count, freq_count = spectra.shape
    blk_count = lax.axis_size("blk")
    step_count = blk_count // 2 + 1
    id_count = channel_ids.shape[0]
    rest = jnp.zeros((-(id_count + step_count + 1) % (8 * LANES),), jnp.int32)
    info = jnp.concatenate([channel_ids, plan[0], lax.axis_index("grp")[None], rest])

    def other_core(block):
        return lax.ppermute(block, "blk", [(i ^ 1, i) for i in range(blk_count)])

    own = whiten_tiles(spectra)
    partner = passed_along(own, "grp", 1)
    near, far = passed_along(own, "blk", -2), passed_along(own, "blk", -4)
    tables = half_lag_tables(freq_count, 1.0 / math.sqrt(2.0 * freq_count * seg_count))

    def stage(sources, arrays, picks, first, output, side=None):
        return correlate(info, id_count, tables, sources, arrays, picks, first, output, step_count, side)

    alone = [((0, None), (0, None))]
    output = stage([own], [own], alone, 0, None, 0)
    output = stage([partner], [own], alone, 0, output, 1)
    last, output = lax.optimization_barrier((own, output))
    swapped = other_core(last)
    for first in range(1, step_count, 4):
        if first == 1:
            near, far, swapped, output = lax.optimization_barrier((near, far, swapped, output))
            pair = jnp.stack([near, far])
            before = (swapped, None)
        else:
            pair, output = lax.optimization_barrier((later, output))
            before = (crossed, 1)
        if first + 4 < step_count:
            later = passed_along(pair, "blk", -4)
        crossed = other_core(pair)
        picks = [((0, before[1]), (2, 0)), ((1, 0),) * 2, ((2, 0), (2, 1)), ((1, 1),) * 2]
        output = stage([own, partner], [before[0], pair, crossed], picks, first, output)
    return output


def on_device(spectra, channel_ids, plan):
    col_count = spectra.shape[0]
    seg_count = spectra.shape[2]
    freq_count = spectra.shape[3]
    whitened = whiten(spectra)
    row_block = lax.all_gather(whitened, "grp", axis=0, tiled=True)
    row_count = row_block.shape[0]
    rotated = jnp.concatenate([row_block[:, seg_count:], -row_block[:, :seg_count]], axis=1)
    paired = jnp.stack([row_block, rotated])
    blk_count = lax.axis_size("blk")
    step_count = blk_count // 2 + 1
    blk_index = lax.axis_index("blk")
    grp_index = lax.axis_index("grp")
    cos_tab, sin_tab = lag_tables(freq_count)
    lag_count = cos_tab.shape[1]
    row_start = blk_index * row_count
    row_ids = lax.dynamic_slice_in_dim(channel_ids, row_start, row_count, 0)
    row_slots = row_start + jnp.arange(row_count, dtype=jnp.int32)
    slot_list = jnp.arange(step_count, dtype=jnp.int32)
    scaling = 1.0 / math.sqrt(2.0 * freq_count * seg_count)

    def correlate_one(offset, columns, output):
        col_start = (blk_index + offset) % blk_count * row_count + grp_index * col_count
        col_ids = lax.dynamic_slice_in_dim(channel_ids, col_start, col_count, 0)
        col_slots = col_start + jnp.arange(col_count, dtype=jnp.int32)
        cross_spec = jnp.einsum(
            "prsf,csf->prcf", paired, columns, preferred_element_type=jnp.float32
        )
        cross_spec = cross_spec.astype(jnp.bfloat16).reshape(2, row_count * col_count, freq_count)
        real_part = jnp.dot(cross_spec[0], cos_tab, preferred_element_type=jnp.float32)
        imag_part = jnp.dot(cross_spec[1], sin_tab, preferred_element_type=jnp.float32)
        orient = (
            jnp.where(row_ids[:, None] < col_ids[None, :], 1.0, -1.0)
            .astype(jnp.float32)
            .reshape(-1, 1)
        )
        keeper = (row_slots[:, None] != col_slots[None, :]).astype(jnp.float32).reshape(-1, 1)
        lagged = ((real_part + orient * imag_part) * (scaling * keeper)).astype(jnp.bfloat16)
        lagged = lagged.reshape(1, 1, 1, row_count, col_count, lag_count)
        out_slot = jnp.sum(slot_list * (plan[0] == offset).astype(jnp.int32))
        return lax.dynamic_update_slice(output, lagged, (0, out_slot, 0, 0, 0, 0))

    output = jnp.zeros((1, step_count, 1, row_count, col_count, lag_count), jnp.bfloat16)

    def advance(offset, carry):
        columns, output = carry
        output = correlate_one(offset, columns, output)
        columns = passed_along(columns, "blk", -1)
        return (columns, output)

    columns, output = lax.fori_loop(0, step_count - 1, advance, (whitened, output))
    output = correlate_one(step_count - 1, columns, output)
    return output


def solution(mesh):
    blk_count, grp_count = mesh.shape["blk"], mesh.shape["grp"]

    def program(spectra, channel_ids, plan):
        col_count = spectra.shape[0] // (blk_count * grp_count)
        fused = col_count == 2 * PACK and grp_count == 2 and blk_count % 8 == 0
        fused = fused and spectra.shape[3] % (4 * LANES) == 0
        return jax.shard_map(
            on_device_fused if fused else on_device,
            mesh=mesh,
            in_specs=(P(("blk", "grp"), None, None, None), P(), P("blk", None)),
            out_specs=P("blk", None, "grp", None, None, None),
            check_vma=False,
        )(spectra, channel_ids, plan)

    return program
```
